128 devices in a mesh: dp: 16 (over y_lo, x, core), tensor: 8 (over y_hi, z).
Axes of the slice: x: 4, y: 4 (y_hi: 2, y_lo: 2; y = y_hi * 2 + y_lo), z: 4, core: 2. Of those that a mesh axis runs over, the one named last changes fastest.
Arguments:
- context: bfloat16 [2048, 180, 768], P(('dp', 'tensor')), may hold values from -6 to 6
- stream: bfloat16 [2048, 180, 768], P(('dp', 'tensor')), may hold values from -6 to 6
- out_weight: bfloat16 [768, 768], replicated, may hold values from -0.21875 to 0.21875
- gain: float32 [768], replicated, may hold values from 0.5 to 1.5
- bias: float32 [768], replicated, may hold values from -3 to 3
- proj_weight: bfloat16 [768, 128], replicated, may hold values from -0.21875 to 0.21875
- query_states: bfloat16 [32, 32, 768], P('dp'), may hold values from -6 to 6
- passage_len: int32 [2048], P(('dp', 'tensor')), may hold values from 45 to 180, as said below
- passage_dest: int32 [2048], P(('dp', 'tensor')), may hold values from 0 to 2047, as said below
- teacher_states: bfloat16 [2048, 212, 1024], P(('dp', 'tensor')), may hold values from -6 to 6
- teacher_query: bfloat16 [1024, 1024], P(None, 'tensor'), may hold values from -0.1875 to 0.1875
- teacher_key: bfloat16 [1024, 1024], P(None, 'tensor'), may hold values from -0.1875 to 0.1875
Outputs:
- loss: float32 [], replicated
- grad_out: float32 [768, 768], replicated
- grad_proj: float32 [768, 128], replicated
- grad_gain: float32 [768], replicated
- grad_bias: float32 [768], replicated
- grad_context: bfloat16 [2048, 180, 768], P(('dp', 'tensor'))
The draws below stay inside these ranges and needn't reach their ends.
Inputs may be any that keep to these rules, and one draw needn't show every extreme that they name: `passage_dest`: A permutation of the pair positions. Passage rows form runs of 16 (run a = i * 8 + t), and so do pair positions; run a sends exactly 16 / 16 of its rows into each pair run j * 8 + t, for every j. `passage_len`: every run of 16 passage rows holds one passage of full length.
All inputs are finite; a program needn't handle non-finite values.
Results may differ from the reference program's by a relative error of at most 0.011.
Values may be sent and summed in bfloat16 or wider, within the bound.
A program may use at most 192 MiB of HBM per device.

```python
import math
import jax
import jax.numpy as jnp
from jax import lax

D = 768
EMB = 128
SEARCH_WORD_SIZE = 32
LP = 180
NPQ = 64
PAIR_DEV = 16
TD = 1024
PAIRS = 2048
PASSAGES = 2048
QUERIES = 32
N_DP = 16
N_TENSOR = 8


def draw_passage_len(key, part):
    key_lengths, key_slots = jax.random.split(jax.random.fold_in(key, 11))
    lengths = jax.random.randint(key_lengths, (PASSAGES // PAIR_DEV, PAIR_DEV), LP // 4, LP + 1)
    full_slot = jax.random.randint(key_slots, (PASSAGES // PAIR_DEV,), 0, PAIR_DEV)
    row_index = jnp.arange(PAIR_DEV, dtype=jnp.int32)[None, :]
    return jnp.where(row_index == full_slot[:, None], LP, lengths).reshape(-1).astype(jnp.int32)


def draw_passage_dest(key, part):
    key_slots, key_rows = jax.random.split(jax.random.fold_in(key, 23))
    per_dest = PAIR_DEV // N_DP
    groups = N_DP * N_TENSOR
    slot_perms = jax.vmap(lambda inner: jax.random.permutation(inner, PAIR_DEV))(jax.random.split(key_slots, groups)).reshape(N_DP, N_TENSOR, PAIR_DEV)
    row_perms = jax.vmap(lambda inner: jax.random.permutation(inner, PAIR_DEV))(jax.random.split(key_rows, groups)).reshape(N_DP, N_TENSOR, PAIR_DEV)
    sender = slot_perms // per_dest
    within = slot_perms % per_dest
    target = jnp.arange(N_DP, dtype=jnp.int32)[:, None, None]
    member = jnp.arange(N_TENSOR, dtype=jnp.int32)[None, :, None]
    position = jnp.arange(PAIR_DEV, dtype=jnp.int32)[None, None, :]
    local_slot = target * per_dest + within
    member_full = jnp.broadcast_to(member, sender.shape)
    local_row = row_perms[sender, member_full, local_slot]
    source_pos = (sender * N_TENSOR + member_full) * PAIR_DEV + local_row
    pair_pos = (target * N_TENSOR + member) * PAIR_DEV + position
    result = jnp.zeros((PAIRS,), jnp.int32).at[source_pos.reshape(-1)].set(jnp.broadcast_to(pair_pos, source_pos.shape).reshape(-1).astype(jnp.int32))
    return result


def steps_of(stream_key, shape, cuts, smallest, high):
    level, own = 1.0, jax.random.fold_in(stream_key, 6)
    for dim, parts in cuts:
        heights = jnp.exp(jax.random.uniform(jax.random.fold_in(own, dim), (parts,), jnp.float32, smallest / len(cuts), high / len(cuts)))
        level = level * jnp.repeat(heights, shape[dim] // parts).reshape([-1 if axis == dim else 1 for axis in range(len(shape))])
    return level


def gaussian(rng, extent, scale, reach, pieces=(), held_as=jnp.bfloat16):
    factor_of = steps_of(rng, extent, pieces, -0.22, 0.18) if pieces else 1.0
    values = jax.random.normal(rng, extent, jnp.float32) * scale * factor_of
    return jnp.minimum(jnp.maximum(values, -reach), reach).astype(held_as)


def setup_inputs(seed: int = 0) -> dict:
    arg_keys = jax.random.split(jax.random.key(seed), 13)
    context = gaussian(arg_keys[0], (PASSAGES, LP, D), 1.0, 6.0, ((0, 128),))
    stream = gaussian(arg_keys[1], (PASSAGES, LP, D), 1.0, 6.0, ((0, 128),))
    out_weight = gaussian(arg_keys[2], (D, D), D ** -0.5, 0.21875)
    gain = jnp.clip(1.0 + 0.1 * jax.random.normal(arg_keys[3], (D,), jnp.float32), 0.5, 1.5)
    bias = gaussian(arg_keys[4], (D,), 0.5, 3.0, (), jnp.float32)
    proj_weight = gaussian(arg_keys[5], (D, EMB), D ** -0.5, 0.21875)
    query_states = gaussian(arg_keys[6], (QUERIES, SEARCH_WORD_SIZE, D), 1.0, 6.0, ((0, 16),))
    passage_len = draw_passage_len(jax.random.fold_in(arg_keys[12], 71), 0)
    passage_dest = draw_passage_dest(jax.random.fold_in(arg_keys[12], 71), 0)
    teacher_states = gaussian(arg_keys[9], (PAIRS, SEARCH_WORD_SIZE + LP, TD), 1.0, 6.0, ((0, 128),))
    teacher_query = gaussian(arg_keys[10], (TD, TD), TD ** -0.5, 0.1875, ((1, 8),))
    teacher_key = gaussian(arg_keys[11], (TD, TD), TD ** -0.5, 0.1875, ((1, 8),))
    return {"context": context, "stream": stream, "out_weight": out_weight, "gain": gain, "bias": bias, "proj_weight": proj_weight, "query_states": query_states, "passage_len": passage_len, "passage_dest": passage_dest, "teacher_states": teacher_states, "teacher_query": teacher_query, "teacher_key": teacher_key}


sharpness_divisor = 0.05
softcap = 10.0
epsilon = 1e-06

def student_forward(context_rows, stream_rows, out_weight, gain, bias, proj_weight):
    summed = stream_rows.astype(jnp.float32) + jnp.einsum('ptd,de->pte', context_rows.astype(jnp.float32), out_weight.astype(jnp.float32))
    centred = summed - lax.optimization_barrier(jnp.mean(summed, axis=-1, keepdims=True))
    inverse = lax.rsqrt(lax.optimization_barrier(jnp.mean(centred * centred, axis=-1, keepdims=True)) + epsilon)
    normed = centred * inverse
    hidden = (normed * gain + bias).astype(jnp.bfloat16)
    embeds = jnp.einsum('ptd,de->pte', hidden.astype(jnp.float32), proj_weight.astype(jnp.float32))
    length = jnp.sqrt(lax.optimization_barrier(jnp.sum(embeds * embeds, axis=-1, keepdims=True)) + epsilon)
    return (hidden, normed, inverse, embeds, length)

def teacher_map(states, teacher_query, teacher_key):
    query_side = jnp.einsum('pqd,de->pqe', states[:, :SEARCH_WORD_SIZE].astype(jnp.float32), teacher_query.astype(jnp.float32)).astype(jnp.bfloat16)
    key_side = jnp.einsum('pkd,de->pke', states[:, SEARCH_WORD_SIZE:].astype(jnp.float32), teacher_key.astype(jnp.float32)).astype(jnp.bfloat16)
    raw_map = jnp.einsum('pqe,pke->pqk', query_side.astype(jnp.float32), key_side.astype(jnp.float32)) / math.sqrt(TD)
    return softcap * jnp.tanh(raw_map / softcap)

def reference(context, stream, out_weight, gain, bias, proj_weight, query_states, passage_len, passage_dest, teacher_states, teacher_query, teacher_key):
    blocks = PASSAGES // PAIR_DEV
    context_blocks = context.reshape(blocks, PAIR_DEV, LP, D)
    stream_blocks = stream.reshape(blocks, PAIR_DEV, LP, D)

    def forward_block(inputs):
        hidden, normed, inverse, embeds, length = student_forward(inputs[0], inputs[1], out_weight, gain, bias, proj_weight)
        return (embeds / length).astype(jnp.bfloat16)
    unit_vecs = lax.map(forward_block, (context_blocks, stream_blocks)).reshape(PASSAGES, LP, EMB)
    source = jnp.zeros((PAIRS,), jnp.int32).at[passage_dest].set(jnp.arange(PASSAGES, dtype=jnp.int32))
    matched_direction_arrays = unit_vecs[source]
    pair_len = passage_len[source]
    teacher = lax.map(lambda states: teacher_map(states, teacher_query, teacher_key), teacher_states.reshape(blocks, PAIR_DEV, SEARCH_WORD_SIZE + LP, TD)).reshape(PAIRS, SEARCH_WORD_SIZE, LP)
    query_embeds = jnp.einsum('nqd,de->nqe', query_states.astype(jnp.float32), proj_weight.astype(jnp.float32))
    query_length = jnp.sqrt(lax.optimization_barrier(jnp.sum(query_embeds * query_embeds, axis=-1, keepdims=True)) + epsilon)
    query_dir = query_embeds / query_length
    query_unit = query_dir.astype(jnp.bfloat16)
    matched_search_rescaled = query_unit[jnp.arange(PAIRS, dtype=jnp.int32) // NPQ]
    learner_raw_ratings = jnp.einsum('hsn,hfn->hsf', matched_search_rescaled.astype(jnp.float32), matched_direction_arrays.astype(jnp.float32)) / sharpness_divisor
    valid = jnp.arange(LP, dtype=jnp.int32)[None, None, :] < pair_len[:, None, None]
    student_exp = jnp.where(valid, jnp.exp(learner_raw_ratings), 0.0)
    student_total = lax.optimization_barrier(jnp.sum(student_exp, axis=-1, keepdims=True))
    learner_likelihood = student_exp / student_total
    student_log = learner_raw_ratings - jnp.log(student_total)
    teacher_exp = jnp.where(valid, jnp.exp(teacher), 0.0)
    teacher_total = lax.optimization_barrier(jnp.sum(teacher_exp, axis=-1, keepdims=True))
    mentor_likelihood = teacher_exp / teacher_total
    teacher_log = teacher - jnp.log(teacher_total)
    diverge = lax.optimization_barrier(jnp.sum(jnp.where(valid, mentor_likelihood * (teacher_log - student_log), 0.0), axis=-1))
    loss = jnp.sum(diverge) / (PAIRS * SEARCH_WORD_SIZE)
    angle_similarity_slope = ((learner_likelihood - mentor_likelihood) / (SEARCH_WORD_SIZE * sharpness_divisor)).astype(jnp.bfloat16)
    unit_grad = jnp.einsum('pqk,pqc->pkc', angle_similarity_slope.astype(jnp.float32), matched_search_rescaled.astype(jnp.float32)).astype(jnp.bfloat16)
    pair_qgrad = jnp.einsum('pqk,pkc->pqc', angle_similarity_slope.astype(jnp.float32), matched_direction_arrays.astype(jnp.float32))
    query_grad = lax.optimization_barrier(jnp.sum(pair_qgrad.reshape(QUERIES, NPQ, SEARCH_WORD_SIZE, EMB), axis=1))
    query_embed_grad = (query_grad - query_dir * lax.optimization_barrier(jnp.sum(query_dir * query_grad, axis=-1, keepdims=True))) / query_length
    proj_query = jnp.einsum('nqd,nqe->de', query_states.astype(jnp.float32), query_embed_grad, precision=lax.Precision.HIGHEST)
    passage_grad = unit_grad[passage_dest].reshape(blocks, PAIR_DEV, LP, EMB)

    def backward_block(carry, inputs):
        wo_grad, proj_grad, gain_grad, bias_grad = carry
        context_rows, stream_rows, unit_rows = inputs
        hidden, normed, inverse, embeds, length = student_forward(context_rows, stream_rows, out_weight, gain, bias, proj_weight)
        direction = embeds / length
        upstream = unit_rows.astype(jnp.float32)
        embed_grad = ((upstream - direction * lax.optimization_barrier(jnp.sum(direction * upstream, axis=-1, keepdims=True))) / length).astype(jnp.bfloat16)
        proj_grad = proj_grad + jnp.einsum('ptd,pte->de', hidden.astype(jnp.float32), embed_grad.astype(jnp.float32))
        hidden_grad = jnp.einsum('pte,de->ptd', embed_grad.astype(jnp.float32), proj_weight.astype(jnp.float32))
        gain_grad = gain_grad + lax.optimization_barrier(jnp.sum(hidden_grad * normed, axis=(0, 1)))
        bias_grad = bias_grad + lax.optimization_barrier(jnp.sum(hidden_grad, axis=(0, 1)))
        scaled = hidden_grad * gain
        summed_grad = (inverse * (scaled - lax.optimization_barrier(jnp.mean(scaled, axis=-1, keepdims=True)) - normed * lax.optimization_barrier(jnp.mean(scaled * normed, axis=-1, keepdims=True)))).astype(jnp.bfloat16)
        wo_grad = wo_grad + jnp.einsum('ptd,pte->de', context_rows.astype(jnp.float32), summed_grad.astype(jnp.float32))
        context_grad = jnp.einsum('pte,de->ptd', summed_grad.astype(jnp.float32), out_weight.astype(jnp.float32)).astype(jnp.bfloat16)
        return ((wo_grad, proj_grad, gain_grad, bias_grad), context_grad)
    start = (jnp.zeros((D, D), jnp.float32), jnp.zeros((D, EMB), jnp.float32), jnp.zeros((D,), jnp.float32), jnp.zeros((D,), jnp.float32))
    totals, context_grads = lax.scan(backward_block, start, (context_blocks, stream_blocks, passage_grad))
    return (loss, totals[0], totals[1] + proj_query, totals[2], totals[3], context_grads.reshape(PASSAGES, LP, D))
```

```python
import jax
import jax.numpy as jnp
from jax import lax
from jax.experimental import pallas as pl
from jax.experimental.pallas import tpu as pltpu
from jax.sharding import PartitionSpec as P

MESH = pl.DeviceIdType.MESH
F32, BF16 = jnp.float32, jnp.bfloat16
EPS = 1e-06
SHARP = 0.05
CAP = 10.0

PD = 16
LP = 180
ROW = 192
D = 768
EMB = 128
TD = 1024
QW = 32
ND, NT = 16, 8
FLAT = PD * ROW
NN = (((1,), (0,)), ((), ()))
NT_DIMS = (((1,), (1,)), ((), ()))
TN_DIMS = (((0,), (0,)), ((), ()))


def mm(a, b, dims=NN):
    return lax.dot_general(a, b, dims, preferred_element_type=F32)


def mm_exact(a, b):
    return lax.dot_general(
        a, b, NN, precision=lax.Precision.HIGHEST, preferred_element_type=F32
    )


def kernel(
    dest_s, len_s, ctx_h, str_h, ts_h, wo, gain, bias, proj, qs, dest_v, wq_h, wk_h,
    gc_h, res_o, gb_o, loss_o,
    ctx_v, str_v, ts_v, c2d, n2d, sg2d, e_s, ee_s, inv_s, il_s, ug, u16,
    wq, wk, maps, stage, rmaps, qbuf, qd_s, qil_s, dinfo, slot_v, slot_s, qgs, qgr, ltb,
    pq_s, cs_s, xq, qm, tm, ar, r0, w1, r1, w2, r2, w3, r3, res,
    sem_in, sem_ts, sem_w, sem_slot, sem_out, sem_a, sem_b, sem_c, sem_d, sem_e, sem_l, sem_g,
):
    dp, tn = lax.axis_index("dp"), lax.axis_index("tensor")
    ylo, x, core = dp // 8, (dp // 2) % 4, dp % 2
    yhi, z = tn // 4, tn % 4
    y = yhi * 2 + ylo

    def dev(y_, x_, core_, z_):
        return ((y_ % 2) * 8 + x_ * 2 + core_, (y_ // 2) * 4 + z_)

    def on_axis(axis, d):
        if axis == "x":
            return dev(y, (x + d) % 4, core, z)
        if axis == "y":
            return dev((y + d) % 4, x, core, z)
        return dev(y, x, core, (z + d) % 4)

    sibling = dev(y, x, 1 - core, z)
    cross = ((dp + 8) % ND, (tn + 4) % NT)

    def fetch_p(p):
        return (
            pltpu.make_async_copy(ctx_h.at[p], ctx_v.at[p], sem_in.at[0, p]),
            pltpu.make_async_copy(str_h.at[p], str_v.at[p], sem_in.at[1, p]),
        )

    def fetch_t(p):
        return pltpu.make_async_copy(ts_h.at[p], ts_v.at[p], sem_ts.at[p])

    @pl.loop(0, PD)
    def _(p):
        for c in fetch_p(p):
            c.start()

    own_w = [
        pltpu.make_async_copy(wq_h, wq.at[tn], sem_w.at[0]),
        pltpu.make_async_copy(wk_h, wk.at[tn], sem_w.at[1]),
    ]
    for c in own_w:
        c.start()

    peers = [((dp + d) % ND, tn) for d in range(1, ND)]
    peers += [(dp, (tn + d) % NT) for d in range(1, NT)]
    peers += [cross]
    barrier = pltpu.get_barrier_semaphore()
    for peer in peers:
        pl.semaphore_signal(barrier, inc=1, device_id=peer, device_id_type=MESH)

    q_in = qs[yhi]
    q_emb = mm(q_in, proj[...])
    q_il = lax.rsqrt(jnp.sum(q_emb * q_emb, axis=-1, keepdims=True) + EPS)
    q_dir = q_emb * q_il
    qd_s[...] = q_dir
    qil_s[...] = jnp.broadcast_to(q_il, (QW, EMB))
    qbuf[dp] = q_dir.astype(BF16)
    dinfo[dp] = dest_v[...]
    maps[...] = jnp.zeros((PD, QW, 256), BF16)

    @pl.loop(0, PD)
    def _(p):
        r = pl.multiple_of(p * ROW + 176, 16)
        for ref in (c2d, n2d, sg2d):
            ref[pl.ds(r, 16), :] = jnp.zeros((16, D), BF16)
        ee_s[pl.ds(r, 16), :] = jnp.zeros((16, EMB), BF16)

    for c in own_w:
        c.wait()
    pl.semaphore_wait(barrier, len(peers))

    started = []

    def rcopy(src, dst, sem, k, to):
        return pltpu.make_async_remote_copy(
            src_ref=src, dst_ref=dst, send_sem=sem.at[0, k], recv_sem=sem.at[1, k],
            device_id=to, device_id_type=MESH,
        )

    def go(copy):
        copy.start()
        started.append(copy)

    def send_all(buf, sem):
        out = []
        for d in range(1, ND):
            c = rcopy(buf.at[dp], buf.at[dp], sem, d - 1, ((dp + d) % ND, tn))
            go(c)
            out.append(c)
        return out

    dcopies = send_all(dinfo, sem_a)
    half = TD // 2
    base = core * half
    wcopies = {}
    counter = [0]

    def rows_of(part):
        if part == "all":
            return base, half
        if part == "hi":
            return base, half // 2
        return base + half // 2, half // 2

    def wsend(name, buf, t_, part, to):
        start, size = rows_of(part)
        view = buf.at[t_, pl.ds(pl.multiple_of(start, 16), size)]
        c = rcopy(view, view, sem_b, counter[0], to)
        counter[0] += 1
        go(c)
        wcopies[name] = c

    zp, zm = on_axis("z", 1), on_axis("z", 3)
    t_zm, t_zp, t_zz = yhi * 4 + (z + 3) % 4, yhi * 4 + (z + 1) % 4, yhi * 4 + (z + 2) % 4

    def flip(t_):
        return (t_ + 4) % NT

    wsend("q_x", wq, tn, "all", cross)
    wsend("q_zp", wq, tn, "all", zp)
    wsend("q_zm", wq, tn, "all", zm)
    wsend("k_zp", wk, tn, "all", zp)
    wsend("k_zm", wk, tn, "all", zm)
    wsend("k_x", wk, tn, "all", cross)
    qcopies = send_all(qbuf, sem_c)

    def got(*names):
        for n in names:
            wcopies[n].wait_recv()

    def step2q():
        got("q_zp", "q_zm", "q_x")
        wsend("q_x_zp", wq, flip(tn), "all", zp)
        wsend("q_x_zm", wq, flip(tn), "all", zm)
        wsend("q_zz_p", wq, t_zm, "hi", zp)
        wsend("q_zz_m", wq, t_zp, "lo", zm)
        wsend("s_q_zm", wq, t_zm, "all", sibling)
        wsend("s_q_zp", wq, t_zp, "all", sibling)
        wsend("s_q_x", wq, flip(tn), "all", sibling)

    def step2k():
        got("k_zp", "k_zm", "k_x")
        wsend("k_zm_x", wk, t_zm, "all", cross)
        wsend("k_zp_x", wk, t_zp, "all", cross)
        wsend("k_zz_p", wk, t_zm, "hi", zp)
        wsend("k_zz_m", wk, t_zp, "lo", zm)
        wsend("s_k_zm", wk, t_zm, "all", sibling)
        wsend("s_k_zp", wk, t_zp, "all", sibling)
        wsend("s_k_x", wk, flip(tn), "all", sibling)

    def step3():
        got("q_x_zp", "q_x_zm")
        wsend("q_xzz_p", wq, flip(t_zm), "hi", zp)
        wsend("q_xzz_m", wq, flip(t_zp), "lo", zm)
        wsend("s_q_xzm", wq, flip(t_zm), "all", sibling)
        wsend("s_q_xzp", wq, flip(t_zp), "all", sibling)
        got("q_zz_p", "q_zz_m")
        wsend("s_q_zz", wq, t_zz, "all", sibling)
        got("k_zz_p", "k_zz_m")
        wsend("k_zz_x", wk, t_zz, "all", cross)
        wsend("s_k_zz", wk, t_zz, "all", sibling)

    def step4():
        got("q_xzz_p", "q_xzz_m")
        wsend("s_q_xzz", wq, flip(t_zz), "all", sibling)
        got("k_zm_x", "k_zp_x")
        wsend("s_k_xzm", wk, flip(t_zm), "all", sibling)
        wsend("s_k_xzp", wk, flip(t_zp), "all", sibling)
        got("k_zz_x")
        wsend("s_k_xzz", wk, flip(t_zz), "all", sibling)

    def forward(ps):
        for p in ps:
            for c in fetch_p(p):
                c.wait()
        xs = [ctx_v[p] for p in ps]
        ss = [mm(v, wo[...]) for v in xs]
        for p, v, s in zip(ps, xs, ss):
            row = pl.ds(pl.multiple_of(p * ROW, 16), LP)
            s = s + str_v[p].astype(F32)
            c = s - jnp.mean(s, axis=-1, keepdims=True)
            inv = lax.rsqrt(jnp.mean(c * c, axis=-1, keepdims=True) + EPS)
            n = c * inv
            h = (n * gain[...] + bias[...]).astype(BF16)
            e = mm(h, proj[...])
            il = lax.rsqrt(jnp.sum(e * e, axis=-1, keepdims=True) + EPS)
            c2d[row, :] = v
            n2d[row, :] = n.astype(BF16)
            inv_s[row, :] = inv
            e_s[row, :] = e
            il_s[row, :] = il
            u16[p] = (e * il).astype(BF16)

    def forward_loop(lo, hi):
        @pl.loop(lo // 2, hi // 2)
        def _(i):
            forward([2 * i, 2 * i + 1])

    @pl.loop(0, PD)
    def _(p):
        fetch_t(p).start()

    forward_loop(0, 6)
    step2q()
    forward_loop(6, 10)
    step2k()
    forward_loop(10, 16)

    for c in dcopies:
        c.wait_recv()
    dest_all = dinfo[:, 0, :]
    lane = lax.broadcasted_iota(jnp.int32, (ND, EMB), 1)
    mine = jnp.logical_and((dest_all // (PD * NT)) == dp, lane < PD)
    slots = jnp.max(jnp.where(mine, dest_all % PD, 0), axis=-1, keepdims=True)
    slot_v[...] = jnp.broadcast_to(slots, (ND, EMB))
    slot_copy = pltpu.make_async_copy(slot_v, slot_s, sem_slot)
    slot_copy.start()

    step3()

    @pl.loop(0, PD)
    def _(p):
        fetch_t(p).wait()
        xq[pl.ds(pl.multiple_of(p * QW, 16), QW), :] = ts_v[p, 0:QW, :]

    step4()
    got("s_q_zm", "s_q_zp", "s_q_x", "s_q_xzm", "s_q_xzp", "s_q_zz", "s_q_xzz")

    @pl.loop(0, NT // 2)
    def _(h):
        w = jnp.concatenate([wq[2 * h], wq[2 * h + 1]], axis=1)
        qm[:, pl.ds(pl.multiple_of(h * 256, 256), 256)] = mm(xq[...], w).astype(BF16)

    got("s_k_zm", "s_k_zp", "s_k_x", "s_k_xzm", "s_k_xzp", "s_k_zz", "s_k_xzz")

    @pl.loop(0, TD // 256)
    def _(b):
        rows = pl.ds(pl.multiple_of(b * 256, 256), 256)
        w = jnp.concatenate([wk[h, rows, :] for h in range(NT)], axis=1)
        tm[:, rows] = mm(qm[...], w, NT_DIMS).astype(BF16)

    @pl.loop(0, PD // 2)
    def _(i):
        for p in (2 * i, 2 * i + 1):
            t_rows = tm[pl.ds(pl.multiple_of(p * QW, 16), QW), :]
            raw = mm(t_rows, ts_v[p, QW : QW + LP, :], NT_DIMS) * (1.0 / 32.0)
            maps[p, :, 0:LP] = raw.astype(BF16)

    slot_copy.wait()
    mcopies = []
    for d in range(1, ND):
        stage[d] = maps[slot_s[(dp + d) % ND, 0]]
    rmaps[dp] = maps[slot_s[dp, 0]]
    for d in range(1, ND):
        c = rcopy(stage.at[d], rmaps.at[dp], sem_d, d - 1, ((dp + d) % ND, tn))
        go(c)
        mcopies.append(c)
    for c in qcopies + mcopies:
        c.wait_recv()

    def score(j, loss):
        r = jnp.int32(0)
        for k in range(PD):
            r = jnp.maximum(r, jnp.where(dest_s[k] // (PD * NT) == j, k, 0))
        q = qbuf[j]
        u = u16[r]
        lg = mm(q, u, NT_DIMS) * (1.0 / SHARP)
        t = CAP * jnp.tanh(rmaps[j][:, 0:LP].astype(F32) * (1.0 / CAP))
        valid = lax.broadcasted_iota(jnp.int32, (QW, LP), 1) < len_s[r]
        s_exp = jnp.where(valid, jnp.exp(lg), 0.0)
        s_tot = jnp.sum(s_exp, axis=-1, keepdims=True)
        s_prob = s_exp / s_tot
        t_exp = jnp.where(valid, jnp.exp(t), 0.0)
        t_tot = jnp.sum(t_exp, axis=-1, keepdims=True)
        t_prob = t_exp / t_tot
        log_ratio = (t - jnp.log(t_tot)) - (lg - jnp.log(s_tot))
        loss = loss + jnp.sum(
            jnp.where(valid, t_prob * log_ratio, 0.0), axis=-1, keepdims=True
        )
        cg = ((s_prob - t_prob) * (1.0 / (QW * SHARP))).astype(BF16)
        ug[j] = mm(cg, q, TN_DIMS).astype(BF16)
        qgs[j, 0:QW, :] = mm(cg, u)
        return loss

    def score2(i, loss):
        return score(2 * i + 1, score(2 * i, loss))

    loss = lax.fori_loop(0, PD // 2, score2, jnp.zeros((QW, 1), F32))
    loss_row = jnp.broadcast_to(jnp.sum(loss, axis=0, keepdims=True), (8, EMB))

    @pl.loop(0, ND)
    def _(j):
        qgs[j, QW : QW + 8, :] = loss_row

    qgr[dp] = qgs[dp]
    gcopies = []
    for d in range(1, ND):
        peer = (dp + d) % ND
        c = rcopy(qgs.at[peer], qgr.at[dp], sem_e, d - 1, (peer, tn))
        go(c)
        gcopies.append(c)

    pgm = mm_exact(gain[...], proj[...].astype(F32)) * (1.0 / D)
    pb = mm_exact(bias[...], proj[...].astype(F32))

    def backward(ps, cs):
        for p in ps:
            row = pl.ds(pl.multiple_of(p * ROW, 16), LP)
            u = ug[dest_s[p] // (PD * NT)].astype(F32)
            e, il = e_s[row, :], il_s[row, :]
            d = e * il
            eg = ((u - d * jnp.sum(d * u, axis=-1, keepdims=True)) * il).astype(BF16)
            ef = eg.astype(F32)
            cs = cs + jnp.sum(ef, axis=0, keepdims=True)
            m1 = jnp.sum(ef * pgm, axis=-1, keepdims=True)
            m2 = jnp.sum(ef * (e - pb), axis=-1, keepdims=True) * (1.0 / D)
            n = mm(eg, proj[...], NT_DIMS) * gain[...]
            sg = inv_s[row, :] * (n - m1 - n2d[row, :].astype(F32) * m2)
            sg2d[row, :] = sg.astype(BF16)
            ee_s[row, :] = eg
        return cs

    cs = lax.fori_loop(
        0, PD // 2, lambda i, cs: backward([2 * i, 2 * i + 1], cs), jnp.zeros((1, EMB), F32)
    )
    cs_s[...] = jnp.broadcast_to(cs, (8, EMB))

    for c in gcopies:
        c.wait_recv()
    total = qgr[0]
    for j in range(1, ND):
        total = total + qgr[j]
    ltb[tn] = total[QW : QW + 8, :]
    lcopies = []
    for d in range(1, NT):
        c = rcopy(ltb.at[tn], ltb.at[tn], sem_l, d - 1, (dp, (tn + d) % NT))
        go(c)
        lcopies.append(c)
    qg, qd = total[0:QW, :], qd_s[...]
    qeg = (qg - qd * jnp.sum(qd * qg, axis=-1, keepdims=True)) * qil_s[...]
    hi = qeg.astype(BF16)
    lo = (qeg - hi.astype(F32)).astype(BF16)
    pq_s[...] = mm(qs[yhi], hi, TN_DIMS) + mm(qs[yhi], lo, TN_DIMS)

    orders = (("x", "y", "z"), ("y", "z", "x"), ("z", "x", "y"))
    place = {"x": x, "y": y, "z": z}

    gcol = jnp.broadcast_to(gain[...], (8, D)).T
    bcol = jnp.broadcast_to(bias[...], (8, D)).T

    def block(b):
        lo_, hi_ = 256 * b, 256 * b + 256
        ar[b, :, 0:D] = mm(c2d[:, lo_:hi_], sg2d[...], TN_DIMS).astype(BF16)
        m = mm(n2d[:, lo_:hi_], ee_s[...], TN_DIMS)
        cs_row = cs_s[0:1, :]
        pr = proj[lo_:hi_, :].astype(F32)
        pg = gcol[lo_:hi_, 0:1] * m + bcol[lo_:hi_, 0:1] * cs_row + pq_s[lo_:hi_, :]
        ar[b, :, D : D + EMB] = pg.astype(BF16)
        gg = jnp.sum(pr * m, axis=-1, keepdims=True)
        gb = jnp.sum(pr * cs_row, axis=-1, keepdims=True)
        ln = lax.broadcasted_iota(jnp.int32, (256, EMB), 1)
        ar[b, :, D + EMB :] = jnp.where(ln == 0, gg, jnp.where(ln == 1, gb, 0.0)).astype(BF16)

    gsem = [0]
    pend = {}

    def gsend(key, src, dst, to):
        c = rcopy(src, dst, sem_g, gsem[0], to)
        gsem[0] += 1
        go(c)
        pend.setdefault(key, []).append(c)

    def gwait(key):
        for c in pend[key]:
            c.wait_recv()

    def my_rows(b):
        return pl.multiple_of(core * 128, 128), pl.multiple_of(place[orders[b][0]] * 32, 32)

    def ds(i, unit, size):
        return pl.ds(pl.multiple_of(i * unit, unit), size)

    def s0(b):
        gsend(("s0", b), ar.at[b, ds(1 - core, 128, 128)], r0.at[b], sibling)

    def s1(b):
        gwait(("s0", b))
        w1[b] = (ar[b, ds(core, 128, 128), :].astype(F32) + r0[b].astype(F32)).astype(BF16)
        a = orders[b][0]
        for d in (2, 1, 3):
            gsend(("s1", b), w1.at[b, ds((place[a] + d) % 4, 32, 32)], r1.at[b, d - 1], on_axis(a, d))

    def s2(b):
        gwait(("s1", b))
        acc = w1[b, ds(place[orders[b][0]], 32, 32), :].astype(F32)
        for d in range(3):
            acc = acc + r1[b, d].astype(F32)
        w2[b] = acc.astype(BF16)
        a = orders[b][1]
        for d in (2, 1, 3):
            gsend(("s2", b), w2.at[b, :, ds((place[a] + d) % 4, 256, 256)], r2.at[b, d - 1], on_axis(a, d))

    def s3(b):
        gwait(("s2", b))
        acc = w2[b, :, ds(place[orders[b][1]], 256, 256)].astype(F32)
        for d in range(3):
            acc = acc + r2[b, d].astype(F32)
        w3[b] = acc.astype(BF16)
        a = orders[b][2]
        for d in (2, 1, 3):
            q = (place[a] + d) % 4
            gsend(
                ("s3", b), w3.at[b, ds(q // 2, 16, 16), ds(q % 2, 128, 128)], r3.at[b, d - 1], on_axis(a, d)
            )

    def spot(b, level):
        p1, p2, p3 = (place[a] for a in orders[b])
        row, rows, col, cols = core * 128, 128, 0, 1024
        if level >= 1:
            row, rows = row + p1 * 32, 32
        if level >= 2:
            col, cols = p2 * 256, 256
        if level >= 3:
            row, rows, col, cols = row + (p3 // 2) * 16, 16, col + (p3 % 2) * 128, 128
        return pl.ds(pl.multiple_of(row, rows), rows), pl.ds(pl.multiple_of(col, min(cols, 1024)), cols)

    def g3(b):
        gwait(("s3", b))
        q = place[orders[b][2]]
        acc = w3[b, ds(q // 2, 16, 16), ds(q % 2, 128, 128)].astype(F32)
        for d in range(3):
            acc = acc + r3[b, d].astype(F32)
        i, k = spot(b, 3)
        res[b, i, k] = acc.astype(BF16)
        for d in (2, 1, 3):
            gsend(("g3", b), res.at[b, i, k], res.at[b, i, k], on_axis(orders[b][2], d))

    def g2(b):
        gwait(("g3", b))
        i, k = spot(b, 2)
        for d in (2, 1, 3):
            gsend(("g2", b), res.at[b, i, k], res.at[b, i, k], on_axis(orders[b][1], d))

    def g1(b):
        gwait(("g2", b))
        i, _ = spot(b, 1)
        for d in (2, 1, 3):
            gsend(("g1", b), res.at[b, i], res.at[b, i], on_axis(orders[b][0], d))

    def g0(b):
        gwait(("g1", b))
        i, _ = spot(b, 0)
        gsend(("g0", b), res.at[b, i], res.at[b, i], sibling)

    def out(b):
        gwait(("g0", b))
        lo_, hi_ = 256 * b, 256 * b + 256
        v = res[b]
        res_o[lo_:hi_, :] = v[:, 0 : D + EMB]
        tr = v[:, D + EMB :].astype(F32).T
        gb_o[:, lo_:hi_] = tr[0:8, :]

    stages = (s0, s1, s2, s3, g3, g2, g1, g0, out)

    def out_copy(p):
        return pltpu.make_async_copy(ctx_v.at[p], gc_h.at[p], sem_out.at[p])

    def context_grad(i):
        @pl.loop(i, i + 1)
        def _(k):
            for p in (2 * k, 2 * k + 1):
                row = pl.ds(pl.multiple_of(p * ROW, 16), LP)
                ctx_v[p] = mm(sg2d[row, :], wo[...], NT_DIMS).astype(BF16)
                out_copy(p).start()

    chunk = 0
    for tick in range(len(stages) + 2):
        for b in range(3):
            k = tick - b
            if k == 0:
                block(b)
            if 0 <= k < len(stages):
                stages[k](b)
        if tick >= 2 and chunk < PD // 2:
            context_grad(chunk)
            chunk += 1

    for c in lcopies:
        c.wait_recv()
    loss_all = ltb[0]
    for t_ in range(1, NT):
        loss_all = loss_all + ltb[t_]
    loss_o[...] = loss_all * (1.0 / (PD * ND * NT * QW))

    @pl.loop(0, PD)
    def _(p):
        out_copy(p).wait()

    for c in started:
        c.wait_send()


def local(
    context, stream, out_weight, gain, bias, proj_weight, query_states, passage_len, passage_dest,
    teacher_states, teacher_query, teacher_key,
):
    dest_v = jnp.pad(passage_dest, (0, EMB - PD))[None, :]
    smem = pl.BlockSpec(memory_space=pltpu.SMEM)
    vmem = pl.BlockSpec(memory_space=pltpu.VMEM)
    hbm = pl.BlockSpec(memory_space=pl.ANY)
    v = pltpu.VMEM
    dma = pltpu.SemaphoreType.DMA
    scratch = [
        v((PD, LP, D), BF16), v((PD, LP, D), BF16), v((PD, QW + LP, TD), BF16),
        v((FLAT, D), BF16), v((FLAT, D), BF16), v((FLAT, D), BF16),
        v((FLAT, EMB), F32), v((FLAT, EMB), BF16), v((FLAT, 1), F32), v((FLAT, 1), F32),
        v((PD, LP, EMB), BF16), v((PD, LP, EMB), BF16),
        v((NT, TD, EMB), BF16), v((NT, TD, EMB), BF16),
        v((PD, QW, 256), BF16), v((ND, QW, 256), BF16), v((ND, QW, 256), BF16),
        v((ND, QW, EMB), BF16), v((QW, EMB), F32), v((QW, EMB), F32),
        v((ND, 1, EMB), jnp.int32), v((ND, EMB), jnp.int32), pltpu.SMEM((ND, EMB), jnp.int32),
        v((ND, QW + 8, EMB), F32), v((ND, QW + 8, EMB), F32), v((NT, 8, EMB), F32),
        v((D, EMB), F32), v((8, EMB), F32),
        v((PD * QW, TD), BF16), v((PD * QW, TD), BF16), v((PD * QW, TD), BF16),
        v((3, 256, 1024), BF16), v((3, 128, 1024), BF16), v((3, 128, 1024), BF16),
        v((3, 3, 32, 1024), BF16), v((3, 32, 1024), BF16), v((3, 3, 32, 256), BF16),
        v((3, 32, 256), BF16), v((3, 3, 16, 128), BF16), v((3, 256, 1024), BF16),
        dma((2, PD)), dma((PD,)), dma((2,)), dma, dma((PD,)),
        dma((2, ND - 1)), dma((2, 40)), dma((2, ND - 1)), dma((2, ND - 1)), dma((2, ND - 1)),
        dma((2, NT - 1)), dma((2, 60)),
    ]
    grad_context, res, gb, loss = pl.pallas_call(
        kernel,
        out_shape=(
            jax.ShapeDtypeStruct((PD, LP, D), BF16),
            jax.ShapeDtypeStruct((D, D + EMB), BF16),
            jax.ShapeDtypeStruct((8, D), F32),
            jax.ShapeDtypeStruct((8, EMB), F32),
        ),
        in_specs=[smem, smem, hbm, hbm, hbm, vmem, vmem, vmem, vmem, vmem, vmem, hbm, hbm],
        out_specs=(hbm, vmem, vmem, vmem),
        scratch_shapes=scratch,
        compiler_params=pltpu.CompilerParams(
            collective_id=0, has_side_effects=True, vmem_limit_bytes=67043328
        ),
        name="distill",
    )(
        passage_dest, passage_len, context, stream, teacher_states, out_weight, gain[None, :],
        bias[None, :], proj_weight, query_states, dest_v, teacher_query, teacher_key,
    )
    return (
        loss[0, 0], res[:, :D].astype(F32), res[:, D:].astype(F32), gb[0], gb[1], grad_context,
    )


def solution(mesh):
    return jax.shard_map(
        local,
        mesh=mesh,
        in_specs=(
            P(("dp", "tensor"), None, None),
            P(("dp", "tensor"), None, None),
            P(),
            P(),
            P(),
            P(),
            P("dp", None, None),
            P(("dp", "tensor")),
            P(("dp", "tensor")),
            P(("dp", "tensor"), None, None),
            P(None, "tensor"),
            P(None, "tensor"),
        ),
        out_specs=(P(), P(), P(), P(), P(), P(("dp", "tensor"), None, None)),
        check_vma=False,
    )
```

```python
import jax
import jax.numpy as jnp
from jax import lax
from jax.experimental import pallas as pl
from jax.experimental.pallas import tpu as pltpu
from jax.sharding import PartitionSpec as P

MESH = pl.DeviceIdType.MESH
F32, BF16 = jnp.float32, jnp.bfloat16
EPS = 1e-06
SHARP = 0.05
CAP = 10.0

PD = 16
LP = 180
FLAT = PD * LP
CH = 288
SUB = 144
NCH = FLAT // CH
D = 768
EMB = 128
TD = 1024
QW = 32
ND, NT = 16, 8
NN = (((1,), (0,)), ((), ()))
NT_DIMS = (((1,), (1,)), ((), ()))
TN_DIMS = (((0,), (0,)), ((), ()))


def mm(a, b, dims=NN):
    return lax.dot_general(a, b, dims, preferred_element_type=F32)


def mm_exact(a, b):
    return lax.dot_general(
        a, b, NN, precision=lax.Precision.HIGHEST, preferred_element_type=F32
    )


class Copy:
    def __init__(self, copy):
        self.copy = copy
        self.received = False
        copy.start()

    def recv(self):
        if not self.received:
            self.copy.wait_recv()
        self.received = True


def kernel(
    dest_s, len_s, ctx_h, str_h, ts_h, wo, gain_r, bias_r, proj, qs, wq_h, wk_h,
    gc_h, res_o, gb_o,
    ctx_v, str_v, ts_v, n2d, e_s, d_s, ug_s, ee_s, inv_s, il_s,
    wq, wk, rawt, maps, stage, rmaps, qbuf, qd_s, qil_s, dinfo, slot_v, slot_s, qtmp, u16, prob, logp, qgs, qgr, ltb,
    pq_s, cs_s, qm, tmf, tm, ar, r0, w1, r1, w2, r2, res,
    sem_in, sem_ts, sem_w, sem_slot, sem_out, sem_a, sem_b, sem_c, sem_d, sem_e, sem_l, sem_g,
):
    sg2d = str_v
    dp, tn = lax.axis_index("dp"), lax.axis_index("tensor")
    ylo, x, core = dp // 8, (dp // 2) % 4, dp % 2
    yhi, z = tn // 4, tn % 4
    y = yhi * 2 + ylo
    gain = gain_r[...].reshape(1, D)
    bias = bias_r[...].reshape(1, D)

    def dev(y_, x_, core_, z_):
        return ((y_ % 2) * 8 + x_ * 2 + core_, (y_ // 2) * 4 + z_)

    def on_axis(axis, d):
        if axis == "x":
            return dev(y, (x + d) % 4, core, z)
        if axis == "y":
            return dev((y + d) % 4, x, core, z)
        return dev(y, x, core, (z + d) % 4)

    sibling = dev(y, x, 1 - core, z)
    cross = ((dp + 8) % ND, (tn + 4) % NT)

    def chunk(i):
        return pl.ds(pl.multiple_of(i * CH, CH), CH)

    def subs(i):
        return [pl.ds(pl.multiple_of(i * CH + k * SUB, SUB), SUB) for k in range(CH // SUB)]

    def fetch(i):
        return (
            pltpu.make_async_copy(ctx_h.at[chunk(i)], ctx_v.at[chunk(i)], sem_in.at[0, i]),
            pltpu.make_async_copy(str_h.at[chunk(i)], str_v.at[chunk(i)], sem_in.at[1, i]),
        )

    def t_rows(i):
        return pl.ds(pl.multiple_of(i * 848, 16), 848)

    def fetch_t(i):
        return pltpu.make_async_copy(ts_h.at[t_rows(i)], ts_v.at[t_rows(i)], sem_ts.at[i])

    @pl.loop(0, NCH)
    def _(i):
        for c in fetch(i):
            c.start()

    own_w = [
        pltpu.make_async_copy(wq_h, wq.at[tn], sem_w.at[0]),
        pltpu.make_async_copy(wk_h, wk.at[tn], sem_w.at[1]),
    ]
    for c in own_w:
        c.start()

    peers = [
        dev((y + dy) % 4, (x + dx) % 4, core, (z + dz) % 4)
        for dy in range(4) for dx in range(4) for dz in range(4)
        if (dy, dx, dz).count(0) in (1, 2)
    ]
    peers += [dev((dp_y + yhi * 2), (x + dx) % 4, 1 - core, z) for dp_y in (ylo, 1 - ylo) for dx in range(4)]
    barrier = pltpu.get_barrier_semaphore()
    for peer in peers:
        pl.semaphore_signal(barrier, inc=1, device_id=peer, device_id_type=MESH)

    q_in = qs[yhi]
    q_emb = mm(q_in, proj[...])
    q_il = lax.rsqrt(jnp.sum(q_emb * q_emb, axis=-1, keepdims=True) + EPS)
    q_dir = q_emb * q_il
    qd_s[...] = q_dir
    qil_s[...] = jnp.broadcast_to(q_il, (QW, EMB))
    qbuf[dp] = q_dir.astype(BF16)
    lane1 = lax.broadcasted_iota(jnp.int32, (1, EMB), 1)
    dest_row = jnp.zeros((1, EMB), jnp.int32)
    for k in range(PD):
        dest_row = jnp.where(lane1 == k, dest_s[k], dest_row)
    dinfo[dp] = dest_row
    maps[...] = jnp.zeros((PD, QW, 256), BF16)

    for c in own_w:
        c.wait()
    pl.semaphore_wait(barrier, len(peers))

    started = []

    def rcopy(src, dst, sem, k, to):
        c = Copy(
            pltpu.make_async_remote_copy(
                src_ref=src, dst_ref=dst, send_sem=sem.at[0, k], recv_sem=sem.at[1, k],
                device_id=to, device_id_type=MESH,
            )
        )
        started.append(c)
        return c

    def finish():
        for c in started:
            c.recv()
        for c in started:
            c.copy.wait_send()

    def send_all(buf, sem):
        out = []
        for d in range(1, ND):
            c = rcopy(buf.at[dp], buf.at[dp], sem, d - 1, ((dp + d) % ND, tn))
            out.append(c)
        return out

    dcopies = send_all(dinfo, sem_a)
    half = TD // 2
    base = core * half
    wcopies = {}
    counter = [0]

    def rows_of(part):
        if part == "all":
            return base, half
        if part == "hi":
            return base, half // 2
        return base + half // 2, half // 2

    def wsend(name, buf, t_, part, to):
        start, size = rows_of(part)
        view = buf.at[t_, pl.ds(pl.multiple_of(start, 16), size)]
        c = rcopy(view, view, sem_b, counter[0], to)
        counter[0] += 1
        wcopies[name] = c

    zp, zm = on_axis("z", 1), on_axis("z", 3)
    t_zm, t_zp, t_zz = yhi * 4 + (z + 3) % 4, yhi * 4 + (z + 1) % 4, yhi * 4 + (z + 2) % 4

    def flip(t_):
        return (t_ + 4) % NT

    wsend("q_x", wq, tn, "all", cross)
    wsend("q_zp", wq, tn, "all", zp)
    wsend("q_zm", wq, tn, "all", zm)
    wsend("k_zp", wk, tn, "all", zp)
    wsend("k_zm", wk, tn, "all", zm)
    wsend("k_x", wk, tn, "all", cross)
    qcopies = send_all(qbuf, sem_c)

    def got(*names):
        for n in names:
            wcopies[n].recv()

    def step2q():
        got("q_zp", "q_zm", "q_x")
        wsend("q_x_zp", wq, flip(tn), "all", zp)
        wsend("q_x_zm", wq, flip(tn), "all", zm)
        wsend("q_zz_p", wq, t_zm, "hi", zp)
        wsend("q_zz_m", wq, t_zp, "lo", zm)
        wsend("s_q_zm", wq, t_zm, "all", sibling)
        wsend("s_q_zp", wq, t_zp, "all", sibling)
        wsend("s_q_x", wq, flip(tn), "all", sibling)

    def step2k():
        got("k_zp", "k_zm", "k_x")
        wsend("k_zm_x", wk, t_zm, "all", cross)
        wsend("k_zp_x", wk, t_zp, "all", cross)
        wsend("k_zz_p", wk, t_zm, "hi", zp)
        wsend("k_zz_m", wk, t_zp, "lo", zm)
        wsend("s_k_zm", wk, t_zm, "all", sibling)
        wsend("s_k_zp", wk, t_zp, "all", sibling)
        wsend("s_k_x", wk, flip(tn), "all", sibling)

    def step3q():
        got("q_x_zp", "q_x_zm")
        wsend("q_xzz_p", wq, flip(t_zm), "hi", zp)
        wsend("q_xzz_m", wq, flip(t_zp), "lo", zm)
        wsend("s_q_xzm", wq, flip(t_zm), "all", sibling)
        wsend("s_q_xzp", wq, flip(t_zp), "all", sibling)
        got("q_zz_p", "q_zz_m")
        wsend("s_q_zz", wq, t_zz, "all", sibling)

    def step3k():
        got("k_zz_p", "k_zz_m")
        wsend("k_zz_x", wk, t_zz, "all", cross)
        wsend("s_k_zz", wk, t_zz, "all", sibling)

    def step4():
        got("q_xzz_p", "q_xzz_m")
        wsend("s_q_xzz", wq, flip(t_zz), "all", sibling)
        got("k_zm_x", "k_zp_x")
        wsend("s_k_xzm", wk, flip(t_zm), "all", sibling)
        wsend("s_k_xzp", wk, flip(t_zp), "all", sibling)

    def step5():
        got("k_zz_x")
        wsend("s_k_xzz", wk, flip(t_zz), "all", sibling)

    def forward(i):
        for c in fetch(i):
            c.wait()
        rows = subs(i)
        sums = [mm(ctx_v[r, :], wo[...]) for r in rows]
        for r, s in zip(rows, sums):
            s = s + str_v[r, :].astype(F32)
            c = s - jnp.mean(s, axis=-1, keepdims=True)
            inv = lax.rsqrt(jnp.mean(c * c, axis=-1, keepdims=True) + EPS)
            n = c * inv
            h = (n * gain + bias).astype(BF16)
            e = mm(h, proj[...])
            il = lax.rsqrt(jnp.sum(e * e, axis=-1, keepdims=True) + EPS)
            n2d[r, :] = n.astype(BF16)
            inv_s[r, :] = inv
            e_s[r, :] = e
            il_s[r, :] = il
            d_s[r, :] = e * il

    def forward_loop(lo, hi):
        @pl.loop(lo, hi)
        def _(i):
            forward(i)

    @pl.loop(0, 4)
    def _(i):
        fetch_t(i).start()

    forward_loop(0, 2)
    step2q()
    forward_loop(2, 4)
    step2k()
    forward_loop(4, 6)
    step3q()
    forward_loop(6, 7)
    step3k()
    forward_loop(7, 8)
    step4()
    forward_loop(8, NCH)

    for c in dcopies:
        c.recv()
    dest_all = dinfo[:, 0, :]
    lane = lax.broadcasted_iota(jnp.int32, (ND, EMB), 1)
    mine = jnp.logical_and((dest_all // (PD * NT)) == dp, lane < PD)
    slots = jnp.max(jnp.where(mine, dest_all % PD, 0), axis=-1, keepdims=True)
    slot_v[...] = jnp.broadcast_to(slots, (ND, EMB))
    slot_copy = pltpu.make_async_copy(slot_v, slot_s, sem_slot)
    slot_copy.start()

    @pl.loop(0, 4)
    def _(i):
        fetch_t(i).wait()

    got("s_q_zm", "s_q_zp", "s_q_x", "s_q_xzm", "s_q_xzp", "s_q_zz", "s_q_xzz")

    @pl.loop(0, NT // 2)
    def _(h):
        w = jnp.concatenate([wq[2 * h], wq[2 * h + 1]], axis=1)
        qm[:, pl.ds(pl.multiple_of(h * 256, 256), 256)] = mm(ts_v[0 : PD * QW, :], w).astype(BF16)

    step5()
    got("s_k_zm", "s_k_zp", "s_k_x", "s_k_xzm", "s_k_xzp", "s_k_zz", "s_k_xzz")

    @pl.loop(0, TD // 256)
    def _(b):
        rows = pl.ds(pl.multiple_of(b * 256, 256), 256)
        w = jnp.concatenate([wk[h, rows, :] for h in range(NT)], axis=1)
        t = mm(qm[...], w, NT_DIMS)
        tmf[2 * b] = t[:, 0:128]
        tmf[2 * b + 1] = t[:, 128:256]

    @pl.loop(0, PD)
    def _(p):
        for k in range(TD // 128):
            part = tmf.at[k][pl.ds(p, QW, stride=PD), :]
            tm[pl.ds(pl.multiple_of(p * QW, QW), QW), 128 * k : 128 * k + 128] = part.astype(BF16)

    @pl.loop(0, NCH)
    def _(i):
        keys = ts_v[pl.ds(pl.multiple_of(PD * QW + i * CH, 16), CH), :]
        full = mm(keys, tm[...], NT_DIMS)
        own = lax.broadcasted_iota(jnp.int32, (CH, PD * QW), 0) % PD
        col = lax.broadcasted_iota(jnp.int32, (CH, PD * QW), 1) // QW
        full = jnp.where(own == col, full, 0.0)
        part = full[:, 0:128] + full[:, 128:256] + full[:, 256:384] + full[:, 384:512]
        part = part + pltpu.roll(part, 64, 1)
        part = part + pltpu.roll(part, 32, 1)
        rawt[chunk(i), :] = part * (1.0 / 32.0)

    @pl.loop(0, PD)
    def _(p):
        pair = rawt[pl.ds(p, LP, stride=PD), :]
        maps[p, :, 0:LP] = pair.T[0:QW, :].astype(BF16)

    slot_copy.wait()
    mcopies = []
    for d in range(1, ND):
        stage[d] = maps[slot_s[(dp + d) % ND, 0]]
    rmaps[dp] = maps[slot_s[dp, 0]]
    for d in range(1, ND):
        c = rcopy(stage.at[d], rmaps.at[dp], sem_d, d - 1, ((dp + d) % ND, tn))
        mcopies.append(c)
    for c in qcopies:
        c.recv()

    def student(p):
        u = d_s[pl.ds(p, LP, stride=PD), :].astype(BF16)
        lg = mm(qbuf[dest_s[p] // (PD * NT)], u, NT_DIMS) * (1.0 / SHARP)
        valid = lax.broadcasted_iota(jnp.int32, (QW, LP), 1) < len_s[p]
        s_exp = jnp.where(valid, jnp.exp(lg), 0.0)
        s_tot = jnp.sum(s_exp, axis=-1, keepdims=True)
        u16[p] = u
        prob[p, :, 0:LP] = s_exp / s_tot
        logp[p, :, 0:LP] = lg - jnp.log(s_tot)

    @pl.loop(0, PD // 2)
    def _(i):
        student(2 * i)
        student(2 * i + 1)

    for c in mcopies:
        c.recv()

    def score(p, loss):
        j = dest_s[p] // (PD * NT)
        t = CAP * jnp.tanh(rmaps[j][:, 0:LP].astype(F32) * (1.0 / CAP))
        valid = lax.broadcasted_iota(jnp.int32, (QW, LP), 1) < len_s[p]
        t_exp = jnp.where(valid, jnp.exp(t), 0.0)
        t_tot = jnp.sum(t_exp, axis=-1, keepdims=True)
        t_prob = t_exp / t_tot
        log_ratio = (t - jnp.log(t_tot)) - logp[p, :, 0:LP]
        loss = loss + jnp.sum(
            jnp.where(valid, t_prob * log_ratio, 0.0), axis=-1, keepdims=True
        )
        cg = ((prob[p, :, 0:LP] - t_prob) * (1.0 / (QW * SHARP))).astype(BF16)
        ug_s[pl.ds(p, LP, stride=PD), :] = mm(cg, qbuf[j], TN_DIMS).astype(BF16).astype(F32)
        qtmp[p] = mm(cg, u16[p])
        return loss

    def score2(i, loss):
        return score(2 * i + 1, score(2 * i, loss))

    loss = lax.fori_loop(0, PD // 2, score2, jnp.zeros((QW, 1), F32))
    loss_row = jnp.broadcast_to(jnp.sum(loss, axis=0, keepdims=True), (8, EMB))

    @pl.loop(0, ND)
    def _(j):
        r = jnp.int32(0)
        for k in range(PD):
            r = jnp.maximum(r, jnp.where(dest_s[k] // (PD * NT) == j, k, 0))
        qgs[j, 0:QW, :] = qtmp[r]
        qgs[j, QW : QW + 8, :] = loss_row

    qgr[dp] = qgs[dp]
    gcopies = []
    for d in range(1, ND):
        peer = (dp + d) % ND
        c = rcopy(qgs.at[peer], qgr.at[dp], sem_e, d - 1, (peer, tn))
        gcopies.append(c)

    pgm = mm_exact(gain, proj[...].astype(F32)) * (1.0 / D)
    pb = mm_exact(bias, proj[...].astype(F32))

    def backward(i, cs):
        for r in subs(i):
            u, e, d, il = ug_s[r, :], e_s[r, :], d_s[r, :], il_s[r, :]
            eg = ((u - d * jnp.sum(d * u, axis=-1, keepdims=True)) * il).astype(BF16)
            ef = eg.astype(F32)
            cs = cs + jnp.sum(ef, axis=0, keepdims=True)
            m1 = jnp.sum(ef * pgm, axis=-1, keepdims=True)
            m2 = jnp.sum(ef * (e - pb), axis=-1, keepdims=True) * (1.0 / D)
            n = mm(eg, proj[...], NT_DIMS) * gain
            sg = inv_s[r, :] * (n - m1 - n2d[r, :].astype(F32) * m2)
            sg2d[r, :] = sg.astype(BF16)
            ee_s[r, :] = eg
        return cs

    cs = lax.fori_loop(0, NCH, backward, jnp.zeros((1, EMB), F32))
    cs_s[...] = jnp.broadcast_to(cs, (8, EMB))

    for c in gcopies:
        c.recv()
    total = qgr[0]
    for j in range(1, ND):
        total = total + qgr[j]
    ltb[tn] = total[QW : QW + 8, :]
    lcopies = []
    for d in range(1, NT):
        c = rcopy(ltb.at[tn], ltb.at[tn], sem_l, d - 1, (dp, (tn + d) % NT))
        lcopies.append(c)
    qg, qd = total[0:QW, :], qd_s[...]
    qeg = (qg - qd * jnp.sum(qd * qg, axis=-1, keepdims=True)) * qil_s[...]
    hi = qeg.astype(BF16)
    lo = (qeg - hi.astype(F32)).astype(BF16)
    pq_s[...] = mm(qs[yhi], hi, TN_DIMS) + mm(qs[yhi], lo, TN_DIMS)

    orders = (("x", "y", "z"), ("y", "z", "x"), ("z", "x", "y"))
    place = {"x": x, "y": y, "z": z}

    gcol = jnp.broadcast_to(gain, (8, D)).T
    bcol = jnp.broadcast_to(bias, (8, D)).T

    def block(b):
        lo_, hi_ = 256 * b, 256 * b + 256
        ar[b, :, 0:D] = mm(ctx_v[:, lo_:hi_], sg2d[...], TN_DIMS).astype(BF16)
        m = mm(n2d[:, lo_:hi_], ee_s[...], TN_DIMS)
        cs_row = cs_s[0:1, :]
        pr = proj[lo_:hi_, :].astype(F32)
        pg = gcol[lo_:hi_, 0:1] * m + bcol[lo_:hi_, 0:1] * cs_row + pq_s[lo_:hi_, :]
        ar[b, :, D : D + EMB] = pg.astype(BF16)
        gg = jnp.sum(pr * m, axis=-1, keepdims=True)
        gb = jnp.sum(pr * cs_row, axis=-1, keepdims=True)
        ln = lax.broadcasted_iota(jnp.int32, (256, EMB), 1)
        ar[b, :, D + EMB :] = jnp.where(ln == 0, gg, jnp.where(ln == 1, gb, 0.0)).astype(BF16)

    gsem = [0]
    pend = {}

    def gsend(key, src, dst, to):
        c = rcopy(src, dst, sem_g, gsem[0], to)
        gsem[0] += 1
        pend.setdefault(key, []).append(c)

    def gwait(key):
        for c in pend[key]:
            c.recv()

    def my_rows(b):
        return pl.multiple_of(core * 128, 128), pl.multiple_of(place[orders[b][0]] * 32, 32)

    def ds(i, unit, size):
        return pl.ds(pl.multiple_of(i * unit, unit), size)

    def s0(b):
        gsend(("s0", b), ar.at[b, ds(1 - core, 128, 128)], r0.at[b], sibling)

    def s1(b):
        gwait(("s0", b))
        w1[b] = (ar[b, ds(core, 128, 128), :].astype(F32) + r0[b].astype(F32)).astype(BF16)
        a = orders[b][0]
        for d in (2, 1, 3):
            gsend(("s1", b), w1.at[b, ds((place[a] + d) % 4, 32, 32)], r1.at[b, d - 1], on_axis(a, d))

    def on_plane(b, d2, d3):
        at = {"x": x, "y": y, "z": z}
        for a, d in zip(orders[b][1:], (d2, d3)):
            at[a] = (at[a] + d) % 4
        return dev(at["y"], at["x"], core, at["z"]), (at[orders[b][1]], at[orders[b][2]])

    def piece(row, col, p2, p3):
        return (
            pl.ds(pl.multiple_of(row + (p3 // 2) * 16, 16), 16),
            pl.ds(pl.multiple_of(col + p2 * 256 + (p3 % 2) * 128, 128), 128),
        )

    shifts = [(d2, d3) for d2 in (2, 1, 3, 0) for d3 in (2, 1, 3, 0) if d2 or d3]

    def s2(b):
        gwait(("s1", b))
        acc = w1[b, ds(place[orders[b][0]], 32, 32), :].astype(F32)
        for d in range(3):
            acc = acc + r1[b, d].astype(F32)
        w2[b] = acc.astype(BF16)
        for k, (d2, d3) in enumerate(shifts):
            to, at = on_plane(b, d2, d3)
            i, j = piece(0, 0, *at)
            gsend(("s2", b), w2.at[b, i, j], r2.at[b, k], to)

    def spot(b):
        return core * 128 + place[orders[b][0]] * 32

    def g2(b):
        gwait(("s2", b))
        at = (place[orders[b][1]], place[orders[b][2]])
        i, j = piece(0, 0, *at)
        acc = w2[b, i, j].astype(F32)
        for k in range(len(shifts)):
            acc = acc + r2[b, k].astype(F32)
        i, j = piece(spot(b), 0, *at)
        res[b, i, j] = acc.astype(BF16)
        for d2, d3 in shifts:
            gsend(("g2", b), res.at[b, i, j], res.at[b, i, j], on_plane(b, d2, d3)[0])

    def g1(b):
        gwait(("g2", b))
        i = pl.ds(pl.multiple_of(spot(b), 32), 32)
        for d in (2, 1, 3):
            gsend(("g1", b), res.at[b, i], res.at[b, i], on_axis(orders[b][0], d))

    def g0(b):
        gwait(("g1", b))
        i = ds(core, 128, 128)
        gsend(("g0", b), res.at[b, i], res.at[b, i], sibling)

    def out(b):
        gwait(("g0", b))
        lo_, hi_ = 256 * b, 256 * b + 256
        v = res[b]
        res_o[lo_:hi_, :] = v[:, 0 : D + EMB]
        tr = v[:, D + EMB :].astype(F32).T
        gb_o[0:2, lo_:hi_] = tr[0:2, :]

    def out_copy(i):
        return pltpu.make_async_copy(ctx_v.at[chunk(i)], gc_h.at[chunk(i)], sem_out.at[i])

    def context_grad(lo, hi):
        @pl.loop(lo, hi)
        def _(i):
            for r in subs(i):
                ctx_v[r, :] = mm(sg2d[r, :], wo[...], NT_DIMS).astype(BF16)
            out_copy(i).start()

    block(0)
    s0(0)
    block(1)
    s1(0)
    s0(1)
    block(2)
    s0(2)
    s1(1)
    s2(0)
    context_grad(0, 2)
    s1(2)
    s2(1)
    context_grad(2, 5)
    g2(0)
    s2(2)
    g2(1)
    context_grad(5, 8)
    g2(2)
    g1(0)
    g1(1)
    context_grad(8, NCH)
    g1(2)
    g0(0)
    g0(1)
    out(0)
    out(1)
    g0(2)
    out(2)

    for c in lcopies:
        c.recv()
    loss_all = ltb[0]
    for t_ in range(1, NT):
        loss_all = loss_all + ltb[t_]
    gb_o[2:3, 0:EMB] = loss_all[0:1, :] * (1.0 / (PD * ND * NT * QW))

    @pl.loop(0, NCH)
    def _(i):
        out_copy(i).wait()

    finish()


def local(
    context, stream, out_weight, gain, bias, proj_weight, query_states, passage_len, passage_dest,
    teacher_states, teacher_query, teacher_key,
):
    flat = lambda a: a.transpose(1, 0, 2).reshape(-1, a.shape[2])
    smem = pl.BlockSpec(memory_space=pltpu.SMEM)
    vmem = pl.BlockSpec(memory_space=pltpu.VMEM)
    hbm = pl.BlockSpec(memory_space=pl.ANY)
    v = pltpu.VMEM
    dma = pltpu.SemaphoreType.DMA
    scratch = [
        v((FLAT, D), BF16), v((FLAT, D), BF16), v((PD * (QW + LP), TD), BF16), v((FLAT, D), BF16),
        v((FLAT, EMB), F32), v((FLAT, EMB), F32), v((FLAT, EMB), F32), v((FLAT, EMB), BF16),
        v((FLAT, 1), F32), v((FLAT, 1), F32),
        v((NT, TD, EMB), BF16), v((NT, TD, EMB), BF16), v((FLAT, EMB), F32),
        v((PD, QW, 256), BF16), v((ND, QW, 256), BF16), v((ND, QW, 256), BF16),
        v((ND, QW, EMB), BF16), v((QW, EMB), F32), v((QW, EMB), F32),
        v((ND, 1, EMB), jnp.int32), v((ND, EMB), jnp.int32), pltpu.SMEM((ND, EMB), jnp.int32),
        v((PD, QW, EMB), F32), v((PD, LP, EMB), BF16), v((PD, QW, 256), F32), v((PD, QW, 256), F32),
        v((ND, QW + 8, EMB), F32), v((ND, QW + 8, EMB), F32), v((NT, 8, EMB), F32),
        v((D, EMB), F32), v((8, EMB), F32),
        v((PD * QW, TD), BF16), v((TD // 128, PD * QW, 128), F32), v((PD * QW, TD), BF16),
        v((3, 256, 1024), BF16), v((3, 128, 1024), BF16), v((3, 128, 1024), BF16),
        v((3, 3, 32, 1024), BF16), v((3, 32, 1024), BF16), v((3, 15, 16, 128), BF16), v((3, 256, 1024), BF16),
        dma((2, NCH)), dma((4,)), dma((2,)), dma, dma((NCH,)),
        dma((2, ND - 1)), dma((2, 40)), dma((2, ND - 1)), dma((2, ND - 1)), dma((2, ND - 1)),
        dma((2, NT - 1)), dma((2, 114)),
    ]
    grad_context, res, gb = pl.pallas_call(
        kernel,
        out_shape=(
            jax.ShapeDtypeStruct((FLAT, D), BF16),
            jax.ShapeDtypeStruct((D, D + EMB), BF16),
            jax.ShapeDtypeStruct((8, D), F32),
        ),
        in_specs=[smem, smem, hbm, hbm, hbm, vmem, vmem, vmem, vmem, vmem, hbm, hbm],
        out_specs=(hbm, vmem, vmem),
        scratch_shapes=scratch,
        compiler_params=pltpu.CompilerParams(
            collective_id=0, has_side_effects=True, vmem_limit_bytes=67043328
        ),
        name="distill",
    )(
        passage_dest, passage_len, flat(context), flat(stream), flat(teacher_states), out_weight, gain,
        bias, proj_weight, query_states, teacher_query, teacher_key,
    )
    return finish_outputs(grad_context, res, gb)


def outputs_kernel(gc_h, res, gb, out_h, wo_o, proj_o, gain_o, bias_o, loss_o, buf, sem):
    def rows(i):
        return pl.ds(pl.multiple_of(i * CH, CH), CH)

    def take(i):
        return pltpu.make_async_copy(gc_h.at[rows(i)], buf.at[rows(i)], sem.at[0, i])

    def give(i):
        return pltpu.make_async_copy(buf.at[rows(i)], out_h.at[rows(i)], sem.at[1, i])

    @pl.loop(0, NCH)
    def _(i):
        take(i).start()

    for k in range(0, D, 256):
        wo_o[k : k + 256, :] = res[k : k + 256, 0:D].astype(F32)
    proj_o[...] = res[:, D:].astype(F32)
    gain_o[...] = gb[0:1, :].reshape(D)
    bias_o[...] = gb[1:2, :].reshape(D)
    loss_o[...] = gb[2:3, 0:1]

    @pl.loop(0, NCH)
    def _(i):
        take(i).wait()
        give(i).start()

    @pl.loop(0, NCH)
    def _(i):
        give(i).wait()


def finish_outputs(grad_context, res, gb):
    vmem = pl.BlockSpec(memory_space=pltpu.VMEM)
    hbm = pl.BlockSpec(memory_space=pl.ANY)
    grad_context, wo_g, proj_g, gain_g, bias_g, loss = pl.pallas_call(
        outputs_kernel,
        out_shape=(
            jax.ShapeDtypeStruct((FLAT, D), BF16),
            jax.ShapeDtypeStruct((D, D), F32),
            jax.ShapeDtypeStruct((D, EMB), F32),
            jax.ShapeDtypeStruct((D,), F32),
            jax.ShapeDtypeStruct((D,), F32),
            jax.ShapeDtypeStruct((1, 1), F32),
        ),
        in_specs=[hbm, vmem, vmem],
        out_specs=(hbm, vmem, vmem, vmem, vmem, vmem),
        scratch_shapes=[pltpu.VMEM((FLAT, D), BF16), pltpu.SemaphoreType.DMA((2, NCH))],
        name="outputs",
    )(grad_context, res, gb)
    return (
        loss.reshape(()), wo_g, proj_g, gain_g, bias_g,
        grad_context.reshape(LP, PD, D).transpose(1, 0, 2),
    )


def solution(mesh):
    return jax.shard_map(
        local,
        mesh=mesh,
        in_specs=(
            P(("dp", "tensor"), None, None),
            P(("dp", "tensor"), None, None),
            P(),
            P(),
            P(),
            P(),
            P("dp", None, None),
            P(("dp", "tensor")),
            P(("dp", "tensor")),
            P(("dp", "tensor"), None, None),
            P(None, "tensor"),
            P(None, "tensor"),
        ),
        out_specs=(P(), P(), P(), P(), P(), P(("dp", "tensor"), None, None)),
        check_vma=False,
    )
```

```python
import jax
import jax.numpy as jnp
from jax import lax
from jax.experimental import pallas as pl
from jax.experimental.pallas import tpu as pltpu
from jax.sharding import PartitionSpec as P

MESH = pl.DeviceIdType.MESH
F32, BF16 = jnp.float32, jnp.bfloat16
EPS = 1e-06
SHARP = 0.05
CAP = 10.0

PD = 16
LP = 180
FLAT = PD * LP
CH = 288
SUB = 144
NCH = FLAT // CH
D = 768
EMB = 128
TD = 1024
QW = 32
ND, NT = 16, 8
NN = (((1,), (0,)), ((), ()))
NT_DIMS = (((1,), (1,)), ((), ()))
TN_DIMS = (((0,), (0,)), ((), ()))


def mm(a, b, dims=NN):
    return lax.dot_general(a, b, dims, preferred_element_type=F32)


def mm_exact(a, b):
    return lax.dot_general(
        a, b, NN, precision=lax.Precision.HIGHEST, preferred_element_type=F32
    )


class Copy:
    def __init__(self, copy):
        self.copy = copy
        self.received = False
        copy.start()

    def recv(self):
        if not self.received:
            self.copy.wait_recv()
        self.received = True


def kernel(
    dest_s, len_s, ctx_h, str_h, ts_h, wo, gain_r, bias_r, proj, qs, wq_h, wk_h,
    gc_h, res_o, gb_o,
    ctx_v, str_v, ts_v, n2d, e_s, d_s, ug_s, ee_s, inv_s, il_s,
    wq, wk, rawt, maps, stage, rmaps, qbuf, qd_s, qil_s, dinfo, slot_v, slot_s, qtmp, u16, prob, logp, qgs, qgr, ltb,
    pq_s, cs_s, qm, tmf, tm, ar, r0, w1, r1, w2, r2, res,
    sem_in, sem_ts, sem_w, sem_slot, sem_out, sem_a, sem_b, sem_c, sem_d, sem_e, sem_l, sem_g,
):
    sg2d = str_v
    dp, tn = lax.axis_index("dp"), lax.axis_index("tensor")
    ylo, x, core = dp // 8, (dp // 2) % 4, dp % 2
    yhi, z = tn // 4, tn % 4
    y = yhi * 2 + ylo
    gain = gain_r[...].reshape(1, D)
    bias = bias_r[...].reshape(1, D)

    def dev(y_, x_, core_, z_):
        return ((y_ % 2) * 8 + x_ * 2 + core_, (y_ // 2) * 4 + z_)

    def on_axis(axis, d):
        if axis == "x":
            return dev(y, (x + d) % 4, core, z)
        if axis == "y":
            return dev((y + d) % 4, x, core, z)
        return dev(y, x, core, (z + d) % 4)

    sibling = dev(y, x, 1 - core, z)
    cross = ((dp + 8) % ND, (tn + 4) % NT)

    def chunk(i):
        return pl.ds(pl.multiple_of(i * CH, CH), CH)

    def subs(i):
        return [pl.ds(pl.multiple_of(i * CH + k * SUB, SUB), SUB) for k in range(CH // SUB)]

    def fetch(i):
        return (
            pltpu.make_async_copy(ctx_h.at[chunk(i)], ctx_v.at[chunk(i)], sem_in.at[0, i]),
            pltpu.make_async_copy(str_h.at[chunk(i)], str_v.at[chunk(i)], sem_in.at[1, i]),
        )

    def t_rows(i):
        return pl.ds(pl.multiple_of(i * 848, 16), 848)

    def fetch_t(i):
        return pltpu.make_async_copy(ts_h.at[t_rows(i)], ts_v.at[t_rows(i)], sem_ts.at[i])

    own_w = [
        pltpu.make_async_copy(wq_h, wq.at[tn], sem_w.at[0]),
        pltpu.make_async_copy(wk_h, wk.at[tn], sem_w.at[1]),
    ]
    for c in own_w:
        c.start()

    @pl.loop(0, NCH)
    def _(i):
        for c in fetch(i):
            c.start()

    peers = [
        dev((y + dy) % 4, (x + dx) % 4, core, (z + dz) % 4)
        for dy in range(4) for dx in range(4) for dz in range(4)
        if (dy, dx, dz).count(0) in (1, 2)
    ]
    peers += [dev((dp_y + yhi * 2), (x + dx) % 4, 1 - core, z) for dp_y in (ylo, 1 - ylo) for dx in range(4)]
    barrier = pltpu.get_barrier_semaphore()
    for peer in peers:
        pl.semaphore_signal(barrier, inc=1, device_id=peer, device_id_type=MESH)

    q_in = qs[yhi]
    q_emb = mm(q_in, proj[...])
    q_il = lax.rsqrt(jnp.sum(q_emb * q_emb, axis=-1, keepdims=True) + EPS)
    q_dir = q_emb * q_il
    qd_s[...] = q_dir
    qil_s[...] = jnp.broadcast_to(q_il, (QW, EMB))
    qbuf[dp] = q_dir.astype(BF16)
    lane1 = lax.broadcasted_iota(jnp.int32, (1, EMB), 1)
    dest_row = jnp.zeros((1, EMB), jnp.int32)
    for k in range(PD):
        dest_row = jnp.where(lane1 == k, dest_s[k], dest_row)
    dinfo[dp] = dest_row
    maps[...] = jnp.zeros((PD, QW, 256), BF16)

    for c in own_w:
        c.wait()
    pl.semaphore_wait(barrier, len(peers))

    started = []

    def rcopy(src, dst, sem, k, to):
        c = Copy(
            pltpu.make_async_remote_copy(
                src_ref=src, dst_ref=dst, send_sem=sem.at[0, k], recv_sem=sem.at[1, k],
                device_id=to, device_id_type=MESH,
            )
        )
        started.append(c)
        return c

    def finish():
        for c in started:
            c.recv()
        for c in started:
            c.copy.wait_send()

    def send_all(buf, sem):
        out = []
        for d in range(1, ND):
            c = rcopy(buf.at[dp], buf.at[dp], sem, d - 1, ((dp + d) % ND, tn))
            out.append(c)
        return out

    half = TD // 2
    base = core * half
    wcopies = {}
    counter = [0]

    def rows_of(part):
        if part == "all":
            return base, half
        if part == "hi":
            return base, half // 2
        return base + half // 2, half // 2

    def wsend(name, buf, t_, part, to):
        start, size = rows_of(part)
        view = buf.at[t_, pl.ds(pl.multiple_of(start, 16), size)]
        c = rcopy(view, view, sem_b, counter[0], to)
        counter[0] += 1
        wcopies[name] = c

    zp, zm = on_axis("z", 1), on_axis("z", 3)
    t_zm, t_zp, t_zz = yhi * 4 + (z + 3) % 4, yhi * 4 + (z + 1) % 4, yhi * 4 + (z + 2) % 4

    def flip(t_):
        return (t_ + 4) % NT

    wsend("q_x", wq, tn, "all", cross)
    wsend("q_zp", wq, tn, "all", zp)
    wsend("q_zm", wq, tn, "all", zm)
    wsend("k_zp", wk, tn, "all", zp)
    wsend("k_zm", wk, tn, "all", zm)
    wsend("k_x", wk, tn, "all", cross)
    dcopies = send_all(dinfo, sem_a)
    qcopies = send_all(qbuf, sem_c)

    def got(*names):
        for n in names:
            wcopies[n].recv()

    def step2q():
        got("q_zp", "q_zm", "q_x")
        wsend("q_x_zp", wq, flip(tn), "all", zp)
        wsend("q_x_zm", wq, flip(tn), "all", zm)
        wsend("q_zz_p", wq, t_zm, "hi", zp)
        wsend("q_zz_m", wq, t_zp, "lo", zm)
        wsend("s_q_zm", wq, t_zm, "all", sibling)
        wsend("s_q_zp", wq, t_zp, "all", sibling)
        wsend("s_q_x", wq, flip(tn), "all", sibling)

    def step2k():
        got("k_zp", "k_zm", "k_x")
        wsend("k_zm_x", wk, t_zm, "all", cross)
        wsend("k_zp_x", wk, t_zp, "all", cross)
        wsend("k_zz_p", wk, t_zm, "hi", zp)
        wsend("k_zz_m", wk, t_zp, "lo", zm)
        wsend("s_k_zm", wk, t_zm, "all", sibling)
        wsend("s_k_zp", wk, t_zp, "all", sibling)
        wsend("s_k_x", wk, flip(tn), "all", sibling)

    def step3q():
        got("q_x_zp", "q_x_zm")
        wsend("q_xzz_p", wq, flip(t_zm), "hi", zp)
        wsend("q_xzz_m", wq, flip(t_zp), "lo", zm)
        wsend("s_q_xzm", wq, flip(t_zm), "all", sibling)
        wsend("s_q_xzp", wq, flip(t_zp), "all", sibling)
        got("q_zz_p", "q_zz_m")
        wsend("s_q_zz", wq, t_zz, "all", sibling)

    def step3k():
        got("k_zz_p", "k_zz_m")
        wsend("k_zz_x", wk, t_zz, "all", cross)
        wsend("s_k_zz", wk, t_zz, "all", sibling)

    def step4():
        got("q_xzz_p", "q_xzz_m")
        wsend("s_q_xzz", wq, flip(t_zz), "all", sibling)
        got("k_zm_x", "k_zp_x")
        wsend("s_k_xzm", wk, flip(t_zm), "all", sibling)
        wsend("s_k_xzp", wk, flip(t_zp), "all", sibling)

    def step5():
        got("k_zz_x")
        wsend("s_k_xzz", wk, flip(t_zz), "all", sibling)

    def forward(i):
        for c in fetch(i):
            c.wait()
        rows = subs(i)
        sums = [mm(ctx_v[r, :], wo[...]) for r in rows]
        for r, s in zip(rows, sums):
            s = s + str_v[r, :].astype(F32)
            c = s - jnp.mean(s, axis=-1, keepdims=True)
            inv = lax.rsqrt(jnp.mean(c * c, axis=-1, keepdims=True) + EPS)
            n = c * inv
            h = (n * gain + bias).astype(BF16)
            e = mm(h, proj[...])
            il = lax.rsqrt(jnp.sum(e * e, axis=-1, keepdims=True) + EPS)
            n2d[r, :] = n.astype(BF16)
            inv_s[r, :] = inv
            e_s[r, :] = e
            il_s[r, :] = il
            d_s[r, :] = e * il

    def forward_loop(lo, hi):
        @pl.loop(lo, hi)
        def _(i):
            forward(i)

    @pl.loop(0, 4)
    def _(i):
        fetch_t(i).start()

    forward_loop(0, 2)
    step2q()
    forward_loop(2, 4)
    step2k()
    forward_loop(4, 6)
    step3q()
    forward_loop(6, 7)
    step3k()
    forward_loop(7, 8)
    step4()
    forward_loop(8, NCH)

    for c in dcopies:
        c.recv()
    dest_all = dinfo[:, 0, :]
    lane = lax.broadcasted_iota(jnp.int32, (ND, EMB), 1)
    mine = jnp.logical_and((dest_all // (PD * NT)) == dp, lane < PD)
    slots = jnp.max(jnp.where(mine, dest_all % PD, 0), axis=-1, keepdims=True)
    slot_v[...] = jnp.broadcast_to(slots, (ND, EMB))
    slot_copy = pltpu.make_async_copy(slot_v, slot_s, sem_slot)
    slot_copy.start()

    @pl.loop(0, 4)
    def _(i):
        fetch_t(i).wait()

    got("s_q_zm", "s_q_zp", "s_q_x", "s_q_xzm", "s_q_xzp", "s_q_zz", "s_q_xzz")

    @pl.loop(0, NT // 2)
    def _(h):
        w = jnp.concatenate([wq[2 * h], wq[2 * h + 1]], axis=1)
        qm[:, pl.ds(pl.multiple_of(h * 256, 256), 256)] = mm(ts_v[0 : PD * QW, :], w).astype(BF16)

    step5()
    got("s_k_zm", "s_k_zp", "s_k_x", "s_k_xzm", "s_k_xzp", "s_k_zz", "s_k_xzz")

    @pl.loop(0, TD // 256)
    def _(b):
        rows = pl.ds(pl.multiple_of(b * 256, 256), 256)
        w = jnp.concatenate([wk[h, rows, :] for h in range(NT)], axis=1)
        t = mm(qm[...], w, NT_DIMS)
        tmf[2 * b] = t[:, 0:128]
        tmf[2 * b + 1] = t[:, 128:256]

    @pl.loop(0, PD)
    def _(p):
        for k in range(TD // 128):
            part = tmf.at[k][pl.ds(p, QW, stride=PD), :]
            tm[pl.ds(pl.multiple_of(p * QW, QW), QW), 128 * k : 128 * k + 128] = part.astype(BF16)

    @pl.loop(0, NCH)
    def _(i):
        keys = ts_v[pl.ds(pl.multiple_of(PD * QW + i * CH, 16), CH), :]
        full = mm(keys, tm[...], NT_DIMS)
        own = lax.broadcasted_iota(jnp.int32, (CH, PD * QW), 0) % PD
        col = lax.broadcasted_iota(jnp.int32, (CH, PD * QW), 1) // QW
        full = jnp.where(own == col, full, 0.0)
        part = full[:, 0:128] + full[:, 128:256] + full[:, 256:384] + full[:, 384:512]
        part = part + pltpu.roll(part, 64, 1)
        part = part + pltpu.roll(part, 32, 1)
        rawt[chunk(i), :] = part * (1.0 / 32.0)

    @pl.loop(0, PD)
    def _(p):
        pair = rawt[pl.ds(p, LP, stride=PD), :]
        maps[p, :, 0:LP] = pair.T[0:QW, :].astype(BF16)

    slot_copy.wait()
    mcopies = []
    for d in range(1, ND):
        stage[d] = maps[slot_s[(dp + d) % ND, 0]]
    rmaps[dp] = maps[slot_s[dp, 0]]
    for d in range(1, ND):
        c = rcopy(stage.at[d], rmaps.at[dp], sem_d, d - 1, ((dp + d) % ND, tn))
        mcopies.append(c)
    for c in qcopies:
        c.recv()

    def student(p):
        u = d_s[pl.ds(p, LP, stride=PD), :].astype(BF16)
        lg = mm(qbuf[dest_s[p] // (PD * NT)], u, NT_DIMS) * (1.0 / SHARP)
        valid = lax.broadcasted_iota(jnp.int32, (QW, LP), 1) < len_s[p]
        s_exp = jnp.where(valid, jnp.exp(lg), 0.0)
        s_tot = jnp.sum(s_exp, axis=-1, keepdims=True)
        u16[p] = u
        prob[p, :, 0:LP] = s_exp / s_tot
        logp[p, :, 0:LP] = lg - jnp.log(s_tot)

    @pl.loop(0, PD // 2)
    def _(i):
        student(2 * i)
        student(2 * i + 1)

    for c in mcopies:
        c.recv()

    def score(p, loss):
        j = dest_s[p] // (PD * NT)
        t = CAP * jnp.tanh(rmaps[j][:, 0:LP].astype(F32) * (1.0 / CAP))
        valid = lax.broadcasted_iota(jnp.int32, (QW, LP), 1) < len_s[p]
        t_exp = jnp.where(valid, jnp.exp(t), 0.0)
        t_tot = jnp.sum(t_exp, axis=-1, keepdims=True)
        t_prob = t_exp / t_tot
        log_ratio = (t - jnp.log(t_tot)) - logp[p, :, 0:LP]
        loss = loss + jnp.sum(
            jnp.where(valid, t_prob * log_ratio, 0.0), axis=-1, keepdims=True
        )
        cg = ((prob[p, :, 0:LP] - t_prob) * (1.0 / (QW * SHARP))).astype(BF16)
        ug_s[pl.ds(p, LP, stride=PD), :] = mm(cg, qbuf[j], TN_DIMS).astype(BF16).astype(F32)
        qtmp[p] = mm(cg, u16[p])
        return loss

    def score2(i, loss):
        return score(2 * i + 1, score(2 * i, loss))

    loss = lax.fori_loop(0, PD // 2, score2, jnp.zeros((QW, 1), F32))
    loss_row = jnp.broadcast_to(jnp.sum(loss, axis=0, keepdims=True), (8, EMB))

    @pl.loop(0, ND)
    def _(j):
        r = jnp.int32(0)
        for k in range(PD):
            r = jnp.maximum(r, jnp.where(dest_s[k] // (PD * NT) == j, k, 0))
        qgs[j, 0:QW, :] = qtmp[r]
        qgs[j, QW : QW + 8, :] = loss_row

    qgr[dp] = qgs[dp]
    gcopies = []
    for d in range(1, ND):
        peer = (dp + d) % ND
        c = rcopy(qgs.at[peer], qgr.at[dp], sem_e, d - 1, (peer, tn))
        gcopies.append(c)

    pgm = mm_exact(gain, proj[...].astype(F32)) * (1.0 / D)
    pb = mm_exact(bias, proj[...].astype(F32))

    def backward(i, cs):
        for r in subs(i):
            u, e, d, il = ug_s[r, :], e_s[r, :], d_s[r, :], il_s[r, :]
            eg = ((u - d * jnp.sum(d * u, axis=-1, keepdims=True)) * il).astype(BF16)
            ef = eg.astype(F32)
            cs = cs + jnp.sum(ef, axis=0, keepdims=True)
            m1 = jnp.sum(ef * pgm, axis=-1, keepdims=True)
            m2 = jnp.sum(ef * (e - pb), axis=-1, keepdims=True) * (1.0 / D)
            n = mm(eg, proj[...], NT_DIMS) * gain
            sg = inv_s[r, :] * (n - m1 - n2d[r, :].astype(F32) * m2)
            sg2d[r, :] = sg.astype(BF16)
            ee_s[r, :] = eg
        return cs

    cs = lax.fori_loop(0, NCH, backward, jnp.zeros((1, EMB), F32))
    cs_s[...] = jnp.broadcast_to(cs, (8, EMB))

    for c in gcopies:
        c.recv()
    total = qgr[0]
    for j in range(1, ND):
        total = total + qgr[j]
    ltb[tn] = total[QW : QW + 8, :]
    lcopies = []
    for d in range(1, NT):
        c = rcopy(ltb.at[tn], ltb.at[tn], sem_l, d - 1, (dp, (tn + d) % NT))
        lcopies.append(c)
    qg, qd = total[0:QW, :], qd_s[...]
    qeg = (qg - qd * jnp.sum(qd * qg, axis=-1, keepdims=True)) * qil_s[...]
    hi = qeg.astype(BF16)
    lo = (qeg - hi.astype(F32)).astype(BF16)
    pq_s[...] = mm(qs[yhi], hi, TN_DIMS) + mm(qs[yhi], lo, TN_DIMS)

    orders = (("x", "y", "z"), ("y", "z", "x"), ("z", "x", "y"))
    place = {"x": x, "y": y, "z": z}

    gcol = jnp.broadcast_to(gain, (8, D)).T
    bcol = jnp.broadcast_to(bias, (8, D)).T

    def block(b):
        lo_, hi_ = 256 * b, 256 * b + 256
        ar[b, :, 0:D] = mm(ctx_v[:, lo_:hi_], sg2d[...], TN_DIMS).astype(BF16)
        m = mm(n2d[:, lo_:hi_], ee_s[...], TN_DIMS)
        cs_row = cs_s[0:1, :]
        pr = proj[lo_:hi_, :].astype(F32)
        pg = gcol[lo_:hi_, 0:1] * m + bcol[lo_:hi_, 0:1] * cs_row + pq_s[lo_:hi_, :]
        ar[b, :, D : D + EMB] = pg.astype(BF16)
        gg = jnp.sum(pr * m, axis=-1, keepdims=True)
        gb = jnp.sum(pr * cs_row, axis=-1, keepdims=True)
        ln = lax.broadcasted_iota(jnp.int32, (256, EMB), 1)
        ar[b, :, D + EMB :] = jnp.where(ln == 0, gg, jnp.where(ln == 1, gb, 0.0)).astype(BF16)

    gsem = [0]
    pend = {}

    def gsend(key, src, dst, to):
        c = rcopy(src, dst, sem_g, gsem[0], to)
        gsem[0] += 1
        pend.setdefault(key, []).append(c)

    def gwait(key):
        for c in pend[key]:
            c.recv()

    def my_rows(b):
        return pl.multiple_of(core * 128, 128), pl.multiple_of(place[orders[b][0]] * 32, 32)

    def ds(i, unit, size):
        return pl.ds(pl.multiple_of(i * unit, unit), size)

    def s0(b):
        gsend(("s0", b), ar.at[b, ds(1 - core, 128, 128)], r0.at[b], sibling)

    def s1(b):
        gwait(("s0", b))
        w1[b] = (ar[b, ds(core, 128, 128), :].astype(F32) + r0[b].astype(F32)).astype(BF16)
        a = orders[b][0]
        for d in (2, 1, 3):
            gsend(("s1", b), w1.at[b, ds((place[a] + d) % 4, 32, 32)], r1.at[b, d - 1], on_axis(a, d))

    def on_plane(b, d2, d3):
        at = {"x": x, "y": y, "z": z}
        for a, d in zip(orders[b][1:], (d2, d3)):
            at[a] = (at[a] + d) % 4
        return dev(at["y"], at["x"], core, at["z"]), (at[orders[b][1]], at[orders[b][2]])

    def piece(row, col, p2, p3):
        return (
            pl.ds(pl.multiple_of(row + (p3 // 2) * 16, 16), 16),
            pl.ds(pl.multiple_of(col + p2 * 256 + (p3 % 2) * 128, 128), 128),
        )

    shifts = [(d2, d3) for d2 in (2, 1, 3, 0) for d3 in (2, 1, 3, 0) if d2 or d3]

    def s2(b):
        gwait(("s1", b))
        acc = w1[b, ds(place[orders[b][0]], 32, 32), :].astype(F32)
        for d in range(3):
            acc = acc + r1[b, d].astype(F32)
        w2[b] = acc.astype(BF16)
        for k, (d2, d3) in enumerate(shifts):
            to, at = on_plane(b, d2, d3)
            i, j = piece(0, 0, *at)
            gsend(("s2", b), w2.at[b, i, j], r2.at[b, k], to)

    def spot(b):
        return core * 128 + place[orders[b][0]] * 32

    def g2(b):
        gwait(("s2", b))
        at = (place[orders[b][1]], place[orders[b][2]])
        i, j = piece(0, 0, *at)
        acc = w2[b, i, j].astype(F32)
        for k in range(len(shifts)):
            acc = acc + r2[b, k].astype(F32)
        i, j = piece(spot(b), 0, *at)
        res[b, i, j] = acc.astype(BF16)
        for d2, d3 in shifts:
            gsend(("g2", b), res.at[b, i, j], res.at[b, i, j], on_plane(b, d2, d3)[0])

    def g1(b):
        gwait(("g2", b))
        i = pl.ds(pl.multiple_of(spot(b), 32), 32)
        for d in (2, 1, 3):
            gsend(("g1", b), res.at[b, i], res.at[b, i], on_axis(orders[b][0], d))

    def g0(b):
        gwait(("g1", b))
        i = ds(core, 128, 128)
        gsend(("g0", b), res.at[b, i], res.at[b, i], sibling)

    def out(b):
        gwait(("g0", b))
        lo_, hi_ = 256 * b, 256 * b + 256
        v = res[b]
        res_o[lo_:hi_, :] = v[:, 0 : D + EMB]
        tr = v[:, D + EMB :].astype(F32).T
        gb_o[0:2, lo_:hi_] = tr[0:2, :]

    def out_copy(i):
        return pltpu.make_async_copy(ctx_v.at[chunk(i)], gc_h.at[chunk(i)], sem_out.at[i])

    def context_grad(lo, hi):
        @pl.loop(lo, hi)
        def _(i):
            for r in subs(i):
                ctx_v[r, :] = mm(sg2d[r, :], wo[...], NT_DIMS).astype(BF16)
            out_copy(i).start()

    block(0)
    s0(0)
    block(1)
    s1(0)
    s0(1)
    block(2)
    s0(2)
    s1(1)
    s2(0)
    context_grad(0, 2)
    s1(2)
    s2(1)
    context_grad(2, 5)
    g2(0)
    s2(2)
    g2(1)
    context_grad(5, 8)
    g2(2)
    g1(0)
    g1(1)
    context_grad(8, NCH)
    g1(2)
    g0(0)
    g0(1)
    out(0)
    out(1)
    g0(2)
    out(2)

    for c in lcopies:
        c.recv()
    loss_all = ltb[0]
    for t_ in range(1, NT):
        loss_all = loss_all + ltb[t_]
    gb_o[2:3, 0:EMB] = loss_all[0:1, :] * (1.0 / (PD * ND * NT * QW))

    @pl.loop(0, NCH)
    def _(i):
        out_copy(i).wait()

    finish()


def local(
    context, stream, out_weight, gain, bias, proj_weight, query_states, passage_len, passage_dest,
    teacher_states, teacher_query, teacher_key,
):
    flat = lambda a: a.transpose(1, 0, 2).reshape(-1, a.shape[2])
    smem = pl.BlockSpec(memory_space=pltpu.SMEM)
    vmem = pl.BlockSpec(memory_space=pltpu.VMEM)
    hbm = pl.BlockSpec(memory_space=pl.ANY)
    v = pltpu.VMEM
    dma = pltpu.SemaphoreType.DMA
    scratch = [
        v((FLAT, D), BF16), v((FLAT, D), BF16), v((PD * (QW + LP), TD), BF16), v((FLAT, D), BF16),
        v((FLAT, EMB), F32), v((FLAT, EMB), F32), v((FLAT, EMB), F32), v((FLAT, EMB), BF16),
        v((FLAT, 1), F32), v((FLAT, 1), F32),
        v((NT, TD, EMB), BF16), v((NT, TD, EMB), BF16), v((FLAT, EMB), F32),
        v((PD, QW, 256), BF16), v((ND, QW, 256), BF16), v((ND, QW, 256), BF16),
        v((ND, QW, EMB), BF16), v((QW, EMB), F32), v((QW, EMB), F32),
        v((ND, 1, EMB), jnp.int32), v((ND, EMB), jnp.int32), pltpu.SMEM((ND, EMB), jnp.int32),
        v((PD, QW, EMB), F32), v((PD, LP, EMB), BF16), v((PD, QW, 256), F32), v((PD, QW, 256), F32),
        v((ND, QW + 8, EMB), F32), v((ND, QW + 8, EMB), F32), v((NT, 8, EMB), F32),
        v((D, EMB), F32), v((8, EMB), F32),
        v((PD * QW, TD), BF16), v((TD // 128, PD * QW, 128), F32), v((PD * QW, TD), BF16),
        v((3, 256, 1024), BF16), v((3, 128, 1024), BF16), v((3, 128, 1024), BF16),
        v((3, 3, 32, 1024), BF16), v((3, 32, 1024), BF16), v((3, 15, 16, 128), BF16), v((3, 256, 1024), BF16),
        dma((2, NCH)), dma((4,)), dma((2,)), dma, dma((NCH,)),
        dma((2, ND - 1)), dma((2, 40)), dma((2, ND - 1)), dma((2, ND - 1)), dma((2, ND - 1)),
        dma((2, NT - 1)), dma((2, 114)),
    ]
    grad_context, res, gb = pl.pallas_call(
        kernel,
        out_shape=(
            jax.ShapeDtypeStruct((FLAT, D), BF16),
            jax.ShapeDtypeStruct((D, D + EMB), BF16),
            jax.ShapeDtypeStruct((8, D), F32),
        ),
        in_specs=[smem, smem, hbm, hbm, hbm, vmem, vmem, vmem, vmem, vmem, hbm, hbm],
        out_specs=(hbm, vmem, vmem),
        scratch_shapes=scratch,
        compiler_params=pltpu.CompilerParams(
            collective_id=0, has_side_effects=True, vmem_limit_bytes=67043328
        ),
        name="distill",
    )(
        passage_dest, passage_len, flat(context), flat(stream), flat(teacher_states), out_weight, gain,
        bias, proj_weight, query_states, teacher_query, teacher_key,
    )
    return finish_outputs(grad_context, res, gb)


def outputs_kernel(gc_h, res, gb, out_h, wo_o, proj_o, gain_o, bias_o, loss_o, buf, sem):
    def rows(i):
        return pl.ds(pl.multiple_of(i * CH, CH), CH)

    def take(i):
        return pltpu.make_async_copy(gc_h.at[rows(i)], buf.at[rows(i)], sem.at[0, i])

    def give(i):
        return pltpu.make_async_copy(buf.at[rows(i)], out_h.at[rows(i)], sem.at[1, i])

    @pl.loop(0, NCH)
    def _(i):
        take(i).start()

    for k in range(0, D, 256):
        wo_o[k : k + 256, :] = res[k : k + 256, 0:D].astype(F32)
    proj_o[...] = res[:, D:].astype(F32)
    gain_o[...] = gb[0:1, :].reshape(D)
    bias_o[...] = gb[1:2, :].reshape(D)
    loss_o[...] = gb[2:3, 0:1]

    @pl.loop(0, NCH)
    def _(i):
        take(i).wait()
        give(i).start()

    @pl.loop(0, NCH)
    def _(i):
        give(i).wait()


def finish_outputs(grad_context, res, gb):
    vmem = pl.BlockSpec(memory_space=pltpu.VMEM)
    hbm = pl.BlockSpec(memory_space=pl.ANY)
    grad_context, wo_g, proj_g, gain_g, bias_g, loss = pl.pallas_call(
        outputs_kernel,
        out_shape=(
            jax.ShapeDtypeStruct((FLAT, D), BF16),
            jax.ShapeDtypeStruct((D, D), F32),
            jax.ShapeDtypeStruct((D, EMB), F32),
            jax.ShapeDtypeStruct((D,), F32),
            jax.ShapeDtypeStruct((D,), F32),
            jax.ShapeDtypeStruct((1, 1), F32),
        ),
        in_specs=[hbm, vmem, vmem],
        out_specs=(hbm, vmem, vmem, vmem, vmem, vmem),
        scratch_shapes=[pltpu.VMEM((FLAT, D), BF16), pltpu.SemaphoreType.DMA((2, NCH))],
        name="outputs",
    )(grad_context, res, gb)
    return (
        loss.reshape(()), wo_g, proj_g, gain_g, bias_g,
        grad_context.reshape(LP, PD, D).transpose(1, 0, 2),
    )


def solution(mesh):
    return jax.shard_map(
        local,
        mesh=mesh,
        in_specs=(
            P(("dp", "tensor"), None, None),
            P(("dp", "tensor"), None, None),
            P(),
            P(),
            P(),
            P(),
            P("dp", None, None),
            P(("dp", "tensor")),
            P(("dp", "tensor")),
            P(("dp", "tensor"), None, None),
            P(None, "tensor"),
            P(None, "tensor"),
        ),
        out_specs=(P(), P(), P(), P(), P(), P(("dp", "tensor"), None, None)),
        check_vma=False,
    )
```
